32 devices in a mesh: ctx: 2 (over core), section: 4 (over y, x), dp: 4 (over z).
Axes of the slice: x: 2, y: 2, z: 4, core: 2. Of those that a mesh axis runs over, the one named last changes fastest.
Arguments:
- conv_input: bfloat16 [4, 4, 256, 5120], P('section', 'dp', 'ctx'), may hold values from -6 to 6
- gate_input: bfloat16 [4, 4, 256, 1024], P('section', 'dp', 'ctx'), may hold values from -6 to 6
- step_input: bfloat16 [4, 4, 256, 16], P('section', 'dp', 'ctx'), may hold values from -7 to 3
- cotangent: bfloat16 [4, 4, 256, 1024], P('section', 'dp', 'ctx'), may hold values from -6 to 6
- conv_weight: float32 [4, 4, 5120], P('section'), may hold values from -3 to 3
- conv_bias: float32 [4, 5120], P('section'), may hold values from -0.5 to 0.5
- step_bias: float32 [4, 16], P('section'), may hold values from -0.5 to 0.5
- decay_log: float32 [4, 16], P('section'), may hold values from -6 to 0.3
- skip_gain: float32 [4, 16], P('section'), may hold values from 0.5 to 1.5
- norm_gain: float32 [4, 1024], P('section'), may hold values from 0.5 to 1.5
Outputs:
- next_input: bfloat16 [4, 4, 256, 1024], P('section', 'dp', 'ctx')
- grad_conv_input: bfloat16 [4, 4, 256, 5120], P('section', 'dp', 'ctx')
- grad_gate_input: bfloat16 [4, 4, 256, 1024], P('section', 'dp', 'ctx')
- grad_step_input: bfloat16 [4, 4, 256, 16], P('section', 'dp', 'ctx')
- kernel_filter_derivative: float32 [4, 4, 5120], P('section')
- grad_conv_bias: float32 [4, 5120], P('section')
- grad_step_bias: float32 [4, 16], P('section')
- grad_decay_log: float32 [4, 16], P('section')
- grad_skip_gain: float32 [4, 16], P('section')
- grad_norm_gain: float32 [4, 1024], P('section')
The draws below stay inside these ranges and needn't reach their ends.
All inputs are finite; a program needn't handle non-finite values.
Results may differ from the reference program's by a relative error of at most 0.0026.
Values may be sent and summed in bfloat16 or wider, within the bound.
A program may use at most 128 MiB of HBM per device.

```python
import math
import jax
import jax.numpy as jnp
from jax import lax

HEADS = 16
HEAD_DIM = 64
STATE = 256
GROUPS = 8
CONV = 4
TOK_DEV = 128
DI = 1024
CH = 5120
SEQ = 256
SECTIONS = 4
REPLICAS = 4


def draw_step_input(key, part):
    keys = jax.random.split(key, 3)
    shape = (SECTIONS, REPLICAS, SEQ, HEADS)
    rough_guess = jnp.clip(0.5 * jax.random.normal(keys[0], shape, jnp.float32), -2.0, 2.0)
    shards = SEQ // TOK_DEV
    initial_offset = jax.random.uniform(keys[1], (SECTIONS, REPLICAS, shards, 1, 1), jnp.float32, -0.7, 0.7)
    initial_offset = jnp.broadcast_to(initial_offset, (SECTIONS, REPLICAS, shards, TOK_DEV, HEADS)).reshape(shape)
    places = jax.random.randint(keys[2], (SECTIONS, REPLICAS, 4), 0, SEQ)
    offset_sequence = jnp.arange(SEQ)[None, None, :, None] == places[:, :, None, :]
    packet_clusters = jnp.any(offset_sequence, axis=-1).astype(jnp.float32)[..., None]
    payload_lines = -4.0 + rough_guess + initial_offset + 4.0 * packet_clusters
    return payload_lines.astype(jnp.bfloat16)


def draw_decay_log(key, part):
    keys = jax.random.split(key, 1)
    lowest = math.log(min(1.0, 50.0 / SEQ))
    highest = math.log(1.25)
    share = jax.random.uniform(keys[0], (SECTIONS, HEADS), jnp.float32)
    payload_lines = lowest + (highest - lowest) * share
    return payload_lines.astype(jnp.float32)


def block_levels(stream_key, extent, cuts, low, top_value):
    level = 1.0
    for dim, parts in cuts:
        steps = jax.random.uniform(jax.random.fold_in(jax.random.fold_in(stream_key, 6), dim), (parts,), jnp.float32, low / len(cuts), top_value / len(cuts))
        level = level * jnp.repeat(jnp.exp(steps), extent[dim] // parts).reshape((-1,) + (1,) * (len(extent) - 1 - dim))
    return level


def noise(key, shape, scale, bound, cuts=(), kind=jnp.bfloat16):
    array = scale * jax.random.normal(key, shape, jnp.float32)
    if cuts:
        array = array * block_levels(key, shape, cuts, -0.22, 0.18)
    return jnp.clip(array, -bound, bound).astype(kind)


def setup_inputs(seed: int = 0) -> dict:
    splits = jax.random.split(jax.random.key(seed), 11)
    conv_input = noise(splits[0], (SECTIONS, REPLICAS, SEQ, CH), 1.0, 6.0, ((0, 4), (1, 4), (2, 2)))
    gate_input = noise(splits[1], (SECTIONS, REPLICAS, SEQ, DI), 1.0, 6.0, ((0, 4), (1, 4), (2, 2)))
    step_input = draw_step_input(jax.random.fold_in(splits[10], 71), 0)
    cotangent = noise(splits[3], (SECTIONS, REPLICAS, SEQ, DI), 1.0, 6.0, ((0, 4), (1, 4), (2, 2)))
    conv_weight = noise(splits[4], (SECTIONS, CONV, CH), CONV ** -0.5, 3.0, ((0, 4),), jnp.float32)
    conv_bias = jnp.clip(jax.random.uniform(splits[5], (SECTIONS, CH), jnp.float32, -0.5, 0.5) * block_levels(splits[5], (SECTIONS, CH), ((0, 4),), -0.4, 0.0), -0.5, 0.5)
    step_bias = jnp.clip(jax.random.uniform(splits[6], (SECTIONS, HEADS), jnp.float32, -0.5, 0.5) * block_levels(splits[6], (SECTIONS, HEADS), ((0, 4),), -0.4, 0.0), -0.5, 0.5)
    decay_log = draw_decay_log(jax.random.fold_in(splits[10], 71), 0)
    skip_gain = jnp.clip(0.5 + 1.0 * jax.random.uniform(splits[8], (SECTIONS, HEADS), jnp.float32) ** block_levels(splits[8], (SECTIONS, HEADS), ((0, 4),), -0.2, 0.2), 0.5, 1.5)
    norm_gain = jnp.clip(1.0 + 0.1 * jax.random.normal(splits[9], (SECTIONS, DI), jnp.float32), 0.5, 1.5)
    return dict(conv_input=conv_input, gate_input=gate_input, step_input=step_input, cotangent=cotangent, conv_weight=conv_weight, conv_bias=conv_bias, step_bias=step_bias, decay_log=decay_log, skip_gain=skip_gain, norm_gain=norm_gain)


HIGH_BOUND = lax.Precision.HIGHEST

def layer(conv_rows, gates, steps, conv_weight, conv_bias, step_bias, decay_log, skip_gain, norm_gain):
    seq = conv_rows.shape[0]
    inner = HEADS * HEAD_DIM
    padded = jnp.concatenate([jnp.zeros((CONV - 1, conv_rows.shape[1]), jnp.float32), conv_rows], 0)
    conv = conv_bias[None, :]
    for tap in range(CONV):
        conv = conv + conv_weight[tap][None, :] * padded[tap:tap + seq]
    mixed = jax.nn.silu(conv)
    reps = HEADS // GROUPS
    xs = mixed[:, :inner].reshape(seq, HEADS, HEAD_DIM)
    b_heads = jnp.repeat(mixed[:, inner:inner + GROUPS * STATE].reshape(seq, GROUPS, STATE), reps, axis=1)
    c_heads = jnp.repeat(mixed[:, inner + GROUPS * STATE:].reshape(seq, GROUPS, STATE), reps, axis=1)
    delta = jax.nn.softplus(steps + step_bias[None, :])
    rate = delta * (-jnp.exp(decay_log))[None, :]
    width = math.gcd(seq, 64)
    count = seq // width
    lower = (jnp.arange(width)[:, None] >= jnp.arange(width)[None, :])[:, :, None]

    def block(state, pieces):
        x_blk, b_blk, c_blk, d_blk, r_blk = pieces
        cum = jnp.cumsum(r_blk, axis=0)
        seg = cum[:, None, :] - cum[None, :, :]
        weight = jnp.exp(jnp.where(lower, seg, -jnp.inf))
        score_matrix = jnp.einsum('thn,shn->tsh', c_blk, b_blk, precision=HIGH_BOUND) * weight
        final_output = jnp.einsum('tsh,shp->thp', score_matrix, x_blk * d_blk[:, :, None], precision=HIGH_BOUND)
        final_output = final_output + jnp.einsum('thn,hpn->thp', c_blk, state, precision=HIGH_BOUND) * jnp.exp(cum)[:, :, None]
        tail = jnp.exp(cum[-1][None, :] - cum) * d_blk
        state = jnp.exp(cum[-1])[:, None, None] * state + jnp.einsum('shp,shn->hpn', x_blk * tail[:, :, None], b_blk, precision=HIGH_BOUND)
        return (state, final_output)
    pieces = (xs.reshape(count, width, HEADS, HEAD_DIM), b_heads.reshape(count, width, HEADS, STATE), c_heads.reshape(count, width, HEADS, STATE), delta.reshape(count, width, HEADS), rate.reshape(count, width, HEADS))
    start = jnp.zeros((HEADS, HEAD_DIM, STATE), jnp.float32)
    _, blocks = lax.scan(block, start, pieces)
    y_all = blocks.reshape(seq, HEADS, HEAD_DIM) + skip_gain[None, :, None] * xs
    gated = y_all.reshape(seq, inner) * jax.nn.silu(gates)
    grouped = gated.reshape(seq, GROUPS, inner // GROUPS)
    normed = grouped * lax.rsqrt(lax.optimization_barrier(jnp.mean(grouped * grouped, axis=-1, keepdims=True)) + 1e-05)
    return normed.reshape(seq, inner) * norm_gain[None, :]

def reference(conv_input, gate_input, step_input, cotangent, conv_weight, conv_bias, step_bias, decay_log, skip_gain, norm_gain):
    pairs = SECTIONS * REPLICAS

    def flatten(arr):
        return arr.reshape((pairs,) + arr.shape[2:])

    def widen(arr):
        return jnp.repeat(arr, REPLICAS, axis=0)

    def single(items):
        rows_in, gates_in, steps_in, cot, w_one, w_two, w_three, w_four, w_five, w_six = items
        final_output, pull = jax.vjp(layer, rows_in.astype(jnp.float32), gates_in.astype(jnp.float32), steps_in.astype(jnp.float32), w_one, w_two, w_three, w_four, w_five, w_six)
        grads = pull(cot.astype(jnp.float32))
        return (final_output.astype(jnp.bfloat16), grads[0].astype(jnp.bfloat16), grads[1].astype(jnp.bfloat16), grads[2].astype(jnp.bfloat16), grads[3], grads[4], grads[5], grads[6], grads[7], grads[8])
    results = lax.map(single, (flatten(conv_input), flatten(gate_input), flatten(step_input), flatten(cotangent), widen(conv_weight), widen(conv_bias), widen(step_bias), widen(decay_log), widen(skip_gain), widen(norm_gain)))
    acts = [item.reshape((SECTIONS, REPLICAS) + item.shape[1:]) for item in results[:4]]
    params = [item.reshape((SECTIONS, REPLICAS) + item.shape[1:]).sum(axis=1) for item in results[4:]]

    def later(grad):
        return jnp.concatenate([grad[1:], jnp.zeros_like(grad[:1])], 0)
    next_input = jnp.concatenate([jnp.zeros_like(acts[0][:1]), acts[0][:-1]], 0)
    return (next_input, later(acts[1]), later(acts[2]), later(acts[3]), params[0], params[1], params[2], params[3], params[4], params[5])
```

```python
import functools
import jax
import jax.numpy as jnp
from jax import lax
from jax.experimental import pallas as pl
from jax.experimental.pallas import tpu as pltpu
from jax.sharding import PartitionSpec as P

HEADS = 16
HEAD_DIM = 64
STATE = 256
GROUPS = 8
CONV = 4


HIGH_BOUND = lax.Precision.HIGHEST


def shifted(block, axis, distance):
    devices = range(lax.axis_size(axis))
    route = [(i - distance, i) for i in devices if i - distance in devices]
    return lax.ppermute(block, axis, route)


def prefix(part, axis, combine, identity):
    count = lax.axis_size(axis)
    place = lax.axis_index(axis)
    ahead = count - 1 - place
    gathered = jax.tree.map(lambda a: lax.all_gather(a, axis), part)
    state = jax.tree.map(lambda a, e: jnp.zeros_like(a) + jnp.asarray(e, a.dtype), part, identity)

    def one(turn, state):
        source = count - 1 - turn
        return combine(
            state, jax.tree.map(lambda a: lax.dynamic_index_in_dim(a, source, 0, False), gathered)
        )

    return lax.fori_loop(0, ahead, one, state)


def conv_mix(extended, taps, initial_offset):
    rows = extended.shape[0] - (CONV - 1)
    total = initial_offset[None, :]
    for tap in range(CONV):
        total = total + taps[tap][None, :] * extended[tap : tap + rows]
    return jax.nn.silu(total)


def split_mix(mixed, steps, step_shift, damping_exponents):
    rows = mixed.shape[0]
    inner = HEADS * HEAD_DIM
    payload_lines = mixed[:, :inner].reshape(rows, GROUPS, HEADS // GROUPS, HEAD_DIM)
    in_maps = mixed[:, inner : inner + GROUPS * STATE].reshape(rows, GROUPS, STATE)
    out_maps = mixed[:, inner + GROUPS * STATE :].reshape(rows, GROUPS, STATE)
    delta = jax.nn.softplus(steps + step_shift[None, :])
    cumulative = jnp.cumsum(delta * (-jnp.exp(damping_exponents))[None, :], axis=0)
    return (payload_lines, in_maps, out_maps, delta, cumulative)


def fragment_condition(extended, steps, taps, initial_offset, step_shift, damping_exponents):
    payload_lines, in_maps, out_maps, delta, cumulative = split_mix(
        conv_mix(extended, taps, initial_offset), steps, step_shift, damping_exponents
    )
    rows = payload_lines.shape[0]
    total = cumulative[-1]
    weight = (jnp.exp(total[None, :] - cumulative) * delta).reshape(rows, GROUPS, HEADS // GROUPS)
    state = jnp.einsum(
        "tgrp,tgn->grpn", payload_lines * weight[..., None], in_maps, precision=HIGH_BOUND
    )
    return (state.reshape(HEADS, HEAD_DIM, STATE), total)


def shard_layer(
    extended,
    gates,
    steps,
    taps,
    initial_offset,
    step_shift,
    damping_exponents,
    skip_values,
    gain_values,
    carried,
):
    payload_lines, in_maps, out_maps, delta, cumulative = split_mix(
        conv_mix(extended, taps, initial_offset), steps, step_shift, damping_exponents
    )
    rows = payload_lines.shape[0]
    reps = HEADS // GROUPS
    lower = (jnp.arange(rows)[:, None] >= jnp.arange(rows)[None, :])[None]
    seg = cumulative.T[:, :, None] - cumulative.T[:, None, :]
    weight = jnp.exp(jnp.where(lower, seg, -jnp.inf)).reshape(GROUPS, reps, rows, rows)
    intersection_maps = jnp.einsum("tgn,sgn->gts", out_maps, in_maps, precision=HIGH_BOUND)
    score_matrix = weight * intersection_maps[:, None]
    scaled_values = payload_lines * delta.reshape(rows, GROUPS, reps)[..., None]
    final_output = jnp.einsum("jzlh,hjzc->ljzc", score_matrix, scaled_values, precision=HIGH_BOUND)
    incoming = jnp.einsum(
        "tgn,grpn->tgrp",
        out_maps,
        carried.reshape(GROUPS, reps, HEAD_DIM, STATE),
        precision=HIGH_BOUND,
    )
    final_output = (
        final_output + incoming * jnp.exp(cumulative).reshape(rows, GROUPS, reps)[..., None]
    )
    final_output = (
        final_output + skip_values.reshape(GROUPS, reps)[None, :, :, None] * payload_lines
    )
    gated = final_output.reshape(rows, GROUPS, -1) * jax.nn.silu(gates).reshape(rows, GROUPS, -1)
    normed = gated * lax.rsqrt(jnp.mean(gated * gated, axis=-1, keepdims=True) + 1e-05)
    return normed.reshape(rows, -1) * gain_values[None, :]


def combine(earlier, later):
    return (earlier[0] * later[0], later[0][:, None] * earlier[1] + later[1])


def shards(
    conv_input,
    gate_input,
    step_input,
    cotangent,
    conv_weight,
    conv_bias,
    step_bias,
    decay_log,
    skip_gain,
    norm_gain,
):
    local_rows = conv_input[0, 0]
    count = local_rows.shape[0]
    taps, initial_offset = (conv_weight[0], conv_bias[0])
    step_shift, damping_exponents = (step_bias[0], decay_log[0])
    skip_values, gain_values = (skip_gain[0], norm_gain[0])
    previous = shifted(local_rows[count - (CONV - 1) :], "ctx", 1)
    extended = jnp.concatenate([previous, local_rows], 0).astype(jnp.float32)
    gates = gate_input[0, 0].astype(jnp.float32)
    steps = step_input[0, 0].astype(jnp.float32)
    (state, total), state_pull = jax.vjp(
        fragment_condition, extended, steps, taps, initial_offset, step_shift, damping_exponents
    )
    decay = jnp.exp(total)
    flat_state = state.reshape(HEADS, HEAD_DIM * STATE)
    unity = (jnp.ones((HEADS,), jnp.float32), jnp.zeros((HEADS, HEAD_DIM * STATE), jnp.float32))

    def advance(index, current):
        return shifted(decay[:, None] * current + flat_state, "ctx", 1)

    incoming = lax.fori_loop(
        0, lax.axis_size("ctx") - 1, advance, jnp.zeros((HEADS, HEAD_DIM * STATE), jnp.float32)
    )
    carried = incoming.reshape(HEADS, HEAD_DIM, STATE)
    final_output, layer_pull = jax.vjp(
        shard_layer,
        extended,
        gates,
        steps,
        taps,
        initial_offset,
        step_shift,
        damping_exponents,
        skip_values,
        gain_values,
        carried,
    )
    forward = shifted(final_output.astype(jnp.bfloat16)[None, None], "section", 1)
    grads = layer_pull(cotangent[0, 0].astype(jnp.float32))
    carry_grad = grads[9].reshape(HEADS, HEAD_DIM * STATE)
    outgoing = prefix((decay, carry_grad), "ctx", combine, unity)[1]
    outgoing_grad = outgoing.reshape(HEADS, HEAD_DIM, STATE)
    total_grad = jnp.sum(outgoing_grad * carried, axis=(1, 2)) * decay
    extra = state_pull((outgoing_grad, total_grad))
    ext_grad = grads[0] + extra[0]
    step_grad = grads[2] + extra[1]
    param_terms = (
        grads[3] + extra[2],
        grads[4] + extra[3],
        grads[5] + extra[4],
        grads[6] + extra[5],
        grads[7],
        grads[8],
    )
    returned = shifted(ext_grad[: CONV - 1], "ctx", -1)
    own_grad = ext_grad[CONV - 1 :]
    row_grad = jnp.concatenate(
        [own_grad[: count - (CONV - 1)], own_grad[count - (CONV - 1) :] + returned], 0
    )
    backward = shifted(
        (
            row_grad.astype(jnp.bfloat16)[None, None],
            grads[1].astype(jnp.bfloat16)[None, None],
            step_grad.astype(jnp.bfloat16)[None, None],
        ),
        "section",
        -1,
    )
    summed = lax.psum(
        (
            param_terms[0],
            param_terms[1],
            param_terms[2],
            param_terms[3],
            param_terms[4],
            param_terms[5],
        ),
        ("ctx", "dp"),
    )
    return (
        forward,
        backward[0],
        backward[1],
        backward[2],
        summed[0][None],
        summed[1][None],
        summed[2][None],
        summed[3][None],
        summed[4][None],
        summed[5][None],
    )


MESH = pl.DeviceIdType.MESH
F32 = jnp.float32
BF16 = jnp.bfloat16
INNER = HEADS * HEAD_DIM
REPS = HEADS // GROUPS
WIDE = REPS * HEAD_DIM
MIX = WIDE + 2 * STATE
HALF = GROUPS // 2
NN = ((1,), (0,))
NT = ((1,), (1,))
TN = ((0,), (0,))


def split(a):
    high = a.astype(BF16)
    return high, (a - high.astype(F32)).astype(BF16)


def dot(a, b, dims):
    return lax.dot_general(a, b, (dims, ((), ())), preferred_element_type=F32)


def dot3(a, b, dims):
    return dot(a[0], b[0], dims) + (dot(a[0], b[1], dims) + dot(a[1], b[0], dims))


def group_columns(g):
    return (
        pl.multiple_of(g * WIDE, 128),
        pl.multiple_of(INNER + g * STATE, 128),
        pl.multiple_of(INNER + (GROUPS + g) * STATE, 128),
    )


def pair_kernel(
    conv_in, gate_in, step_in, cot_in, w_ref, b_ref, sb_ref, dl_ref, sk_ref, ng_ref,
    nxt, gconv, ggate, gstep, gtap, gcb, gsb, gdl, gsk, gng,
    uin, steps, upad, zpad, mix, dsl, dtc, sigc, ratec, cumc, cumr, ddt, drate, small,
    stage_c, stage_o, stage_s, step_parts, partial, final, zeros,
    own_sem, xs_sem, xr_sem, st_sem, conv_sem, gate_sem, next_sem, dstep_sem,
    ps_sem, pr_sem, fin_sem, zero_sem,
):
    core = lax.axis_index("ctx")
    sec = lax.axis_index("section")
    dp = lax.axis_index("dp")
    nsec = lax.axis_size("section")
    ndp = lax.axis_size("dp")
    tok = conv_in.shape[2]
    seq = 2 * tok
    other = 1 - core

    def place(c, s, d):
        return {"ctx": c, "section": s, "dp": d}

    def remote(src, dst, send, recv, c, s, d):
        return pltpu.make_async_remote_copy(
            src_ref=src, dst_ref=dst, send_sem=send, recv_sem=recv,
            device_id=place(c, s, d), device_id_type=MESH,
        )

    after = lax.rem(sec + 1, nsec)
    before = lax.rem(sec + nsec - 1, nsec)
    barrier = pltpu.get_barrier_semaphore()

    def greet(c, s, d):
        pl.semaphore_signal(barrier, inc=1, device_id=place(c, s, d), device_id_type=MESH)

    greet(other, sec, dp)
    for c in range(2):
        greet(c, after, dp)
        greet(c, before, dp)
    for k in range(1, ndp):
        greet(core, sec, lax.rem(dp + k, ndp))

    def pieces(g):
        xc, bc, cc = group_columns(g)
        return (
            (conv_in.at[0, 0, :, pl.ds(xc, WIDE)], 0, WIDE),
            (conv_in.at[0, 0, :, pl.ds(bc, STATE)], WIDE, STATE),
            (conv_in.at[0, 0, :, pl.ds(cc, STATE)], WIDE + STATE, STATE),
            (gate_in.at[0, 0, :, pl.ds(xc, WIDE)], MIX, WIDE),
            (cot_in.at[0, 0, :, pl.ds(xc, WIDE)], MIX + WIDE, WIDE),
        )

    mine = pl.ds(pl.multiple_of(core * tok, tok), tok)
    theirs = pl.ds(pl.multiple_of(other * tok, tok), tok)
    own_step = pltpu.make_async_copy(step_in.at[0, 0], steps.at[core], st_sem.at[0])
    own_step.start()

    def fetch(j, _):
        for src, off, width in pieces(core * HALF + j):
            pltpu.make_async_copy(
                src, uin.at[j, mine, pl.ds(off, width)], own_sem.at[j]
            ).start()
        return 0

    lax.fori_loop(0, HALF, fetch, 0)
    zeros[...] = jnp.zeros_like(zeros)
    partial[dp] = jnp.zeros(partial.shape[1:], F32)
    upad[0:8, :] = jnp.zeros((8, MIX), F32)
    zpad[seq : seq + 8, :] = jnp.zeros((8, MIX), F32)
    for ref in (dtc, sigc, ratec, ddt, drate, small):
        ref[...] = jnp.zeros_like(ref)
    pl.semaphore_wait(barrier, 1 + 4 + (ndp - 1))
    step_copy = remote(
        step_in.at[0, 0], steps.at[core], st_sem.at[1], st_sem.at[2], other, sec, dp
    )
    step_copy.start()

    def exchange(j, _):
        for src, off, width in pieces(other * HALF + j):
            remote(
                src, uin.at[j, mine, pl.ds(off, width)], xs_sem.at[j], xr_sem.at[j], other, sec, dp
            ).start()
        return 0

    lax.fori_loop(0, HALF, exchange, 0)

    @pl.when(sec == 0)
    def _():
        pltpu.make_async_copy(zeros, nxt.at[0, 0], zero_sem.at[0]).start()

    @pl.when(sec == nsec - 1)
    def _():
        for part in range(5):
            pltpu.make_async_copy(
                zeros, gconv.at[0, 0, :, pl.ds(part * INNER, INNER)], zero_sem.at[1]
            ).start()
        pltpu.make_async_copy(zeros, ggate.at[0, 0], zero_sem.at[2]).start()

    own_step.wait()
    step_copy.wait()
    raw = steps[...].astype(F32).reshape(seq, HEADS) + sb_ref[...]
    delta = jnp.maximum(raw, 0.0) + jnp.log1p(jnp.exp(-jnp.abs(raw)))
    dtc[:, 0:HEADS] = delta
    sigc[:, 0:HEADS] = jax.nn.sigmoid(raw)
    ratec[:, 0:HEADS] = delta * (-jnp.exp(dl_ref[...]))
    rows2 = lax.broadcasted_iota(jnp.int32, (seq, seq), 0)
    cols2 = lax.broadcasted_iota(jnp.int32, (seq, seq), 1)
    ones_low = jnp.where(rows2 >= cols2, 1.0, 0.0).astype(BF16)
    rate = ratec[...]
    r_hi, r_rest = rate.astype(BF16), rate - rate.astype(BF16).astype(F32)
    r_mid, r_lo = split(r_rest)
    cumulative = dot(ones_low, r_hi, NN) + (dot(ones_low, r_mid, NN) + dot(ones_low, r_lo, NN))
    cumc[...] = cumulative
    cumr[...] = cumulative.T

    def group(j, _):
        g = core * HALF + j
        cols = group_columns(g)
        pltpu.make_async_copy(uin.at[j, mine], uin.at[j, mine], own_sem.at[j]).wait()
        remote(uin.at[j, mine], uin.at[j, theirs], xs_sem.at[j], xr_sem.at[j], other, sec, dp).wait()
        blocks = [(0, cols[0])]
        for base, col in ((WIDE, cols[1]), (WIDE + STATE, cols[2])):
            for part in range(STATE // 128):
                blocks.append((base + part * 128, pl.multiple_of(col + part * 128, 128)))

        for off, col in blocks:
            here = slice(off, off + 128)
            upad[8 : 8 + seq, here] = uin[j, :, here].astype(F32)
            z = b_ref[:, pl.ds(col, 128)]
            for k in range(CONV):
                z = z + w_ref[0, pl.ds(k, 1), pl.ds(col, 128)] * upad[5 + k : 5 + k + seq, here]
            s = jax.nn.sigmoid(z)
            mix[:, here] = z * s
            dsl[:, here] = s * (1.0 + z * (1.0 - s))

        lane = lax.broadcasted_iota(jnp.int32, (seq, 128), 1)
        lane1 = lax.broadcasted_iota(jnp.int32, (1, 128), 1)
        lane16 = lax.broadcasted_iota(jnp.int32, (1, HEADS), 1)
        row = lax.broadcasted_iota(jnp.int32, (seq, seq), 0)
        column = lax.broadcasted_iota(jnp.int32, (seq, seq), 1)
        first = lane < HEAD_DIM

        def pick(ref, h):
            return jnp.sum(jnp.where(lane == h, ref[...], 0.0), axis=1, keepdims=True)

        def pick1(ref, h):
            return jnp.sum(jnp.where(lane16 == h, ref[...], 0.0), axis=1, keepdims=True)

        x = mix[:, 0:WIDE]
        bmap = split(mix[:, WIDE : WIDE + STATE])
        cmap = split(mix[:, WIDE + STATE : MIX])
        h0 = g * REPS
        dt2 = jnp.where(first, pick(dtc, h0), pick(dtc, h0 + 1))
        skip2 = jnp.where(first[0:1], pick1(sk_ref, h0), pick1(sk_ref, h0 + 1))
        xs = x * dt2
        xs_p = split(xs)
        scores = dot3(cmap, bmap, NT)
        decay, mixed, ys = [], [], []
        for r in range(REPS):
            seg = pick(cumc, h0 + r) - cumr[pl.ds(h0 + r, 1), :]
            w = jnp.exp(jnp.where(row >= column, seg, -jnp.inf))
            a = scores * w
            a_p = split(a)
            decay.append(w)
            mixed.append((a, a_p))
            ys.append(dot3(a_p, xs_p, NN))
        y = jnp.where(first, ys[0], ys[1]) + skip2 * x
        gate = uin[j, :, MIX : MIX + WIDE].astype(F32)
        cot = uin[j, :, MIX + WIDE : MIX + 2 * WIDE].astype(F32)
        gain = ng_ref[:, pl.ds(cols[0], WIDE)]
        s = jax.nn.sigmoid(gate)
        act = gate * s
        gated = y * act
        scale = lax.rsqrt(jnp.mean(gated * gated, axis=1, keepdims=True) + 1e-05)
        normed = gated * scale
        stage_o[j, :, 0:WIDE] = (normed * gain).astype(BF16)
        dn = cot * gain
        dgated = scale * (dn - normed * jnp.mean(dn * normed, axis=1, keepdims=True))
        dy = dgated * act
        stage_o[j, :, WIDE : 2 * WIDE] = (dgated * y * (s * (1.0 + gate * (1.0 - s)))).astype(BF16)

        @pl.when(sec < nsec - 1)
        def _():
            for t in range(2):
                remote(
                    stage_o.at[j, pl.ds(t * tok, tok), pl.ds(0, WIDE)],
                    nxt.at[0, 0, :, pl.ds(cols[0], WIDE)],
                    next_sem.at[0], next_sem.at[1], t, sec + 1, dp,
                ).start()

        @pl.when(sec > 0)
        def _():
            for t in range(2):
                remote(
                    stage_o.at[j, pl.ds(t * tok, tok), pl.ds(WIDE, WIDE)],
                    ggate.at[0, 0, :, pl.ds(cols[0], WIDE)],
                    gate_sem.at[0], gate_sem.at[1], t, sec - 1, dp,
                ).start()

        partial[dp, j, 5:6, 0:WIDE] = jnp.sum(cot * normed, axis=0, keepdims=True)
        dyx = jnp.sum(dy * x, axis=0, keepdims=True)
        dscore = jnp.zeros((seq, seq), F32)
        dxs = []
        upper = jnp.where(row <= column, 1.0, 0.0).astype(BF16)
        dy_p = split(dy)
        for r in range(REPS):
            own = first if r == 0 else jnp.logical_not(first)
            dyr_p = split(jnp.where(own, dy, 0.0))
            da = dot3(dyr_p, xs_p, NT)
            dscore = dscore + da * decay[r]
            p = split(da * mixed[r][0])
            later = dot(upper, p[0], NN) + dot(upper, p[1], NN)
            dr = jnp.sum(jnp.where(row > column, later, 0.0), axis=1, keepdims=True)
            drate[...] += jnp.where(lane == h0 + r, dr, 0.0)
            dxs.append(dot3(mixed[r][1], dy_p, TN))
            total = jnp.sum(jnp.where(own[0:1], dyx, 0.0), axis=1, keepdims=True)
            small[2:3, :] += jnp.where(lane1 == h0 + r, total, 0.0)
        dxs = jnp.where(first, dxs[0], dxs[1])
        dxx = dxs * x
        ddt[...] += jnp.where(
            lane == h0, jnp.sum(jnp.where(first, dxx, 0.0), axis=1, keepdims=True), 0.0
        ) + jnp.where(
            lane == h0 + 1, jnp.sum(jnp.where(first, 0.0, dxx), axis=1, keepdims=True), 0.0
        )
        ds_p = split(dscore)
        zpad[0:seq, 0:WIDE] = (skip2 * dy + dxs * dt2) * dsl[:, 0:WIDE]
        zpad[0:seq, WIDE : WIDE + STATE] = dot3(ds_p, cmap, TN) * dsl[:, WIDE : WIDE + STATE]
        zpad[0:seq, WIDE + STATE : MIX] = dot3(ds_p, bmap, NN) * dsl[:, WIDE + STATE : MIX]
        for off, col in blocks:
            here = slice(off, off + 128)
            dz = zpad[0:seq, here]
            du = jnp.zeros((seq, 128), F32)
            for k in range(CONV):
                du = du + w_ref[0, pl.ds(k, 1), pl.ds(col, 128)] * zpad[3 - k : 3 - k + seq, here]
                partial[dp, j, pl.ds(k, 1), here] = jnp.sum(
                    dz * upad[5 + k : 5 + k + seq, here], axis=0, keepdims=True
                )
            partial[dp, j, pl.ds(4, 1), here] = jnp.sum(dz, axis=0, keepdims=True)
            stage_c[j, :, here] = du.astype(BF16)

        @pl.when(sec > 0)
        def _():
            for t in range(2):
                for off, width, col in (
                    (0, WIDE, cols[0]), (WIDE, STATE, cols[1]), (WIDE + STATE, STATE, cols[2])
                ):
                    remote(
                        stage_c.at[j, pl.ds(t * tok, tok), pl.ds(off, width)],
                        gconv.at[0, 0, :, pl.ds(col, width)],
                        conv_sem.at[0], conv_sem.at[1], t, sec - 1, dp,
                    ).start()

        for k in range(1, ndp):
            to = lax.rem(dp + k, ndp)
            remote(
                partial.at[dp, j], partial.at[dp, j], ps_sem.at[to], pr_sem.at[dp], core, sec, to
            ).start()
        return 0

    lax.fori_loop(0, HALF, group, 0)

    damp = jnp.exp(dl_ref[...])
    dr16 = drate[:, 0:HEADS]
    dstep = (ddt[:, 0:HEADS] - dr16 * damp) * sigc[:, 0:HEADS]
    small[0:1, 0:HEADS] = jnp.sum(dstep, axis=0, keepdims=True)
    small[1:2, 0:HEADS] = jnp.sum(dr16 * ratec[:, 0:HEADS], axis=0, keepdims=True)
    stage_s[...] = jnp.zeros_like(stage_s)
    stage_s[:, 0:HEADS] = dstep.astype(BF16)

    @pl.when(sec > 0)
    def _():
        for t in range(2):
            remote(
                stage_s.at[pl.ds(t * tok, tok)], step_parts.at[core],
                dstep_sem.at[2], dstep_sem.at[core], t, sec - 1, dp,
            ).start()

    partial[dp, HALF, :, 0:128] = small[...]
    for k in range(1, ndp):
        to = lax.rem(dp + k, ndp)
        remote(
            partial.at[dp, HALF], partial.at[dp, HALF], ps_sem.at[to], pr_sem.at[dp], core, sec, to
        ).start()
    for k in range(1, ndp):
        to = lax.rem(dp + k, ndp)
        remote(partial.at[dp], partial.at[to], ps_sem.at[to], pr_sem.at[to], core, sec, to).wait()
    total = partial[0]
    for k in range(1, ndp):
        total = total + partial[k]
    final[core] = total
    halves = remote(final.at[core], final.at[core], fin_sem.at[0], fin_sem.at[1], other, sec, dp)
    halves.start()
    remote(final.at[core], final.at[other], fin_sem.at[0], fin_sem.at[1], other, sec, dp).wait()
    for g in range(GROUPS):
        c, j = g // HALF, g % HALF
        gng[0:1, g * WIDE : (g + 1) * WIDE] = final[c, j, 5:6, 0:WIDE]
        for off, width, col in (
            (0, WIDE, g * WIDE),
            (WIDE, STATE, INNER + g * STATE),
            (WIDE + STATE, STATE, INNER + (GROUPS + g) * STATE),
        ):
            gtap[0, :, col : col + width] = final[c, j, 0:CONV, off : off + width]
            gcb[0:1, col : col + width] = final[c, j, CONV : CONV + 1, off : off + width]
    for at, ref in enumerate((gsb, gdl, gsk)):
        ref[...] = final[0, HALF, at : at + 1, 0:HEADS] + final[1, HALF, at : at + 1, 0:HEADS]

    @pl.when(sec == 0)
    def _():
        pltpu.make_async_copy(zeros, nxt.at[0, 0], zero_sem.at[0]).wait()

    @pl.when(sec > 0)
    def _():
        low = sec - 1
        remote(stage_c, stage_c, conv_sem.at[0], conv_sem.at[1], core, low, dp).wait_send()
        half_o = stage_o.at[:, :, pl.ds(0, WIDE)]
        remote(half_o, half_o, gate_sem.at[0], gate_sem.at[1], core, low, dp).wait_send()
        remote(stage_s, stage_s, dstep_sem.at[2], dstep_sem.at[0], core, low, dp).wait_send()
        remote(
            nxt.at[0, 0], nxt.at[0, 0], next_sem.at[0], next_sem.at[1], core, low, dp
        ).wait_recv()

    @pl.when(sec == nsec - 1)
    def _():
        whole = gconv.at[0, 0]
        pltpu.make_async_copy(whole, whole, zero_sem.at[1]).wait()
        pltpu.make_async_copy(zeros, ggate.at[0, 0], zero_sem.at[2]).wait()
        gstep[...] = jnp.zeros_like(gstep)

    @pl.when(sec < nsec - 1)
    def _():
        high = sec + 1
        half_o = stage_o.at[:, :, pl.ds(0, WIDE)]
        remote(half_o, half_o, next_sem.at[0], next_sem.at[1], core, high, dp).wait_send()
        for c in range(2):
            part = step_parts.at[c]
            remote(part, part, dstep_sem.at[2], dstep_sem.at[c], core, high, dp).wait_recv()
        gstep[0, 0] = (step_parts[0].astype(F32) + step_parts[1].astype(F32))[:, 0:HEADS].astype(BF16)
        whole = ggate.at[0, 0]
        remote(whole, whole, gate_sem.at[0], gate_sem.at[1], core, high, dp).wait_recv()
        whole = gconv.at[0, 0]
        remote(whole, whole, conv_sem.at[0], conv_sem.at[1], core, high, dp).wait_recv()


def paired(
    conv_input, gate_input, step_input, cotangent, conv_weight,
    conv_bias, step_bias, decay_log, skip_gain, norm_gain,
):
    tok = conv_input.shape[2]
    seq = 2 * tok
    ndp = lax.axis_size("dp")
    hbm = pl.BlockSpec(memory_space=pl.ANY)
    vmem = pl.BlockSpec(memory_space=pltpu.VMEM)
    like = lambda a, kind: jax.ShapeDtypeStruct(a.shape, kind)
    scratch = [
        pltpu.VMEM((HALF, seq, MIX + 2 * WIDE), BF16),
        pltpu.VMEM((2, tok, HEADS), BF16),
        pltpu.VMEM((seq + 8, MIX), F32),
        pltpu.VMEM((seq + 8, MIX), F32),
        pltpu.VMEM((seq, MIX), F32),
        pltpu.VMEM((seq, MIX), F32),
        pltpu.VMEM((seq, 128), F32),
        pltpu.VMEM((seq, 128), F32),
        pltpu.VMEM((seq, 128), F32),
        pltpu.VMEM((seq, 128), F32),
        pltpu.VMEM((128, seq), F32),
        pltpu.VMEM((seq, 128), F32),
        pltpu.VMEM((seq, 128), F32),
        pltpu.VMEM((8, 128), F32),
        pltpu.VMEM((HALF, seq, MIX), BF16),
        pltpu.VMEM((HALF, seq, 2 * WIDE), BF16),
        pltpu.VMEM((seq, 128), BF16),
        pltpu.VMEM((2, tok, 128), BF16),
        pltpu.VMEM((ndp, HALF + 1, 8, MIX), F32),
        pltpu.VMEM((2, HALF + 1, 8, MIX), F32),
        pltpu.VMEM((tok, INNER), BF16),
        pltpu.SemaphoreType.DMA((HALF,)),
        pltpu.SemaphoreType.DMA((HALF,)),
        pltpu.SemaphoreType.DMA((HALF,)),
        pltpu.SemaphoreType.DMA((3,)),
        pltpu.SemaphoreType.DMA((2,)),
        pltpu.SemaphoreType.DMA((2,)),
        pltpu.SemaphoreType.DMA((2,)),
        pltpu.SemaphoreType.DMA((3,)),
        pltpu.SemaphoreType.DMA((ndp,)),
        pltpu.SemaphoreType.DMA((ndp,)),
        pltpu.SemaphoreType.DMA((2,)),
        pltpu.SemaphoreType.DMA((3,)),
    ]
    return tuple(
        pl.pallas_call(
            pair_kernel,
            name="mixer_tick",
            in_specs=[hbm] * 4 + [vmem] * 6,
            out_specs=[hbm] * 3 + [vmem] * 7,
            out_shape=[
                like(gate_input, BF16),
                like(conv_input, BF16),
                like(gate_input, BF16),
                like(step_input, BF16),
                like(conv_weight, F32),
                like(conv_bias, F32),
                like(step_bias, F32),
                like(decay_log, F32),
                like(skip_gain, F32),
                like(norm_gain, F32),
            ],
            scratch_shapes=scratch,
            compiler_params=pltpu.CompilerParams(collective_id=0, has_side_effects=True),
        )(
            conv_input, gate_input, step_input, cotangent, conv_weight,
            conv_bias, step_bias, decay_log, skip_gain, norm_gain,
        )
    )


def solution(mesh):
    in_specs = (
        P("section", "dp", "ctx", None),
        P("section", "dp", "ctx", None),
        P("section", "dp", "ctx", None),
        P("section", "dp", "ctx", None),
        P("section", None, None),
        P("section", None),
        P("section", None),
        P("section", None),
        P("section", None),
        P("section", None),
    )
    out_specs = (
        P("section", "dp", "ctx", None),
        P("section", "dp", "ctx", None),
        P("section", "dp", "ctx", None),
        P("section", "dp", "ctx", None),
        P("section", None, None),
        P("section", None),
        P("section", None),
        P("section", None),
        P("section", None),
        P("section", None),
    )
    body = paired if mesh.shape["ctx"] == 2 else shards
    return jax.shard_map(body, mesh=mesh, in_specs=in_specs, out_specs=out_specs, check_vma=False)
```

```python
import functools
import jax
import jax.numpy as jnp
from jax import lax
from jax.experimental import pallas as pl
from jax.experimental.pallas import tpu as pltpu
from jax.sharding import PartitionSpec as P

HEADS = 16
HEAD_DIM = 64
STATE = 256
GROUPS = 8
CONV = 4


HIGH_BOUND = lax.Precision.HIGHEST


def shifted(block, axis, distance):
    devices = range(lax.axis_size(axis))
    route = [(i - distance, i) for i in devices if i - distance in devices]
    return lax.ppermute(block, axis, route)


def prefix(part, axis, combine, identity):
    count = lax.axis_size(axis)
    place = lax.axis_index(axis)
    ahead = count - 1 - place
    gathered = jax.tree.map(lambda a: lax.all_gather(a, axis), part)
    state = jax.tree.map(lambda a, e: jnp.zeros_like(a) + jnp.asarray(e, a.dtype), part, identity)

    def one(turn, state):
        source = count - 1 - turn
        return combine(
            state, jax.tree.map(lambda a: lax.dynamic_index_in_dim(a, source, 0, False), gathered)
        )

    return lax.fori_loop(0, ahead, one, state)


def conv_mix(extended, taps, initial_offset):
    rows = extended.shape[0] - (CONV - 1)
    total = initial_offset[None, :]
    for tap in range(CONV):
        total = total + taps[tap][None, :] * extended[tap : tap + rows]
    return jax.nn.silu(total)


def split_mix(mixed, steps, step_shift, damping_exponents):
    rows = mixed.shape[0]
    inner = HEADS * HEAD_DIM
    payload_lines = mixed[:, :inner].reshape(rows, GROUPS, HEADS // GROUPS, HEAD_DIM)
    in_maps = mixed[:, inner : inner + GROUPS * STATE].reshape(rows, GROUPS, STATE)
    out_maps = mixed[:, inner + GROUPS * STATE :].reshape(rows, GROUPS, STATE)
    delta = jax.nn.softplus(steps + step_shift[None, :])
    cumulative = jnp.cumsum(delta * (-jnp.exp(damping_exponents))[None, :], axis=0)
    return (payload_lines, in_maps, out_maps, delta, cumulative)


def fragment_condition(extended, steps, taps, initial_offset, step_shift, damping_exponents):
    payload_lines, in_maps, out_maps, delta, cumulative = split_mix(
        conv_mix(extended, taps, initial_offset), steps, step_shift, damping_exponents
    )
    rows = payload_lines.shape[0]
    total = cumulative[-1]
    weight = (jnp.exp(total[None, :] - cumulative) * delta).reshape(rows, GROUPS, HEADS // GROUPS)
    state = jnp.einsum(
        "tgrp,tgn->grpn", payload_lines * weight[..., None], in_maps, precision=HIGH_BOUND
    )
    return (state.reshape(HEADS, HEAD_DIM, STATE), total)


def shard_layer(
    extended,
    gates,
    steps,
    taps,
    initial_offset,
    step_shift,
    damping_exponents,
    skip_values,
    gain_values,
    carried,
):
    payload_lines, in_maps, out_maps, delta, cumulative = split_mix(
        conv_mix(extended, taps, initial_offset), steps, step_shift, damping_exponents
    )
    rows = payload_lines.shape[0]
    reps = HEADS // GROUPS
    lower = (jnp.arange(rows)[:, None] >= jnp.arange(rows)[None, :])[None]
    seg = cumulative.T[:, :, None] - cumulative.T[:, None, :]
    weight = jnp.exp(jnp.where(lower, seg, -jnp.inf)).reshape(GROUPS, reps, rows, rows)
    intersection_maps = jnp.einsum("tgn,sgn->gts", out_maps, in_maps, precision=HIGH_BOUND)
    score_matrix = weight * intersection_maps[:, None]
    scaled_values = payload_lines * delta.reshape(rows, GROUPS, reps)[..., None]
    final_output = jnp.einsum("jzlh,hjzc->ljzc", score_matrix, scaled_values, precision=HIGH_BOUND)
    incoming = jnp.einsum(
        "tgn,grpn->tgrp",
        out_maps,
        carried.reshape(GROUPS, reps, HEAD_DIM, STATE),
        precision=HIGH_BOUND,
    )
    final_output = (
        final_output + incoming * jnp.exp(cumulative).reshape(rows, GROUPS, reps)[..., None]
    )
    final_output = (
        final_output + skip_values.reshape(GROUPS, reps)[None, :, :, None] * payload_lines
    )
    gated = final_output.reshape(rows, GROUPS, -1) * jax.nn.silu(gates).reshape(rows, GROUPS, -1)
    normed = gated * lax.rsqrt(jnp.mean(gated * gated, axis=-1, keepdims=True) + 1e-05)
    return normed.reshape(rows, -1) * gain_values[None, :]


def combine(earlier, later):
    return (earlier[0] * later[0], later[0][:, None] * earlier[1] + later[1])


def shards(
    conv_input,
    gate_input,
    step_input,
    cotangent,
    conv_weight,
    conv_bias,
    step_bias,
    decay_log,
    skip_gain,
    norm_gain,
):
    local_rows = conv_input[0, 0]
    count = local_rows.shape[0]
    taps, initial_offset = (conv_weight[0], conv_bias[0])
    step_shift, damping_exponents = (step_bias[0], decay_log[0])
    skip_values, gain_values = (skip_gain[0], norm_gain[0])
    previous = shifted(local_rows[count - (CONV - 1) :], "ctx", 1)
    extended = jnp.concatenate([previous, local_rows], 0).astype(jnp.float32)
    gates = gate_input[0, 0].astype(jnp.float32)
    steps = step_input[0, 0].astype(jnp.float32)
    (state, total), state_pull = jax.vjp(
        fragment_condition, extended, steps, taps, initial_offset, step_shift, damping_exponents
    )
    decay = jnp.exp(total)
    flat_state = state.reshape(HEADS, HEAD_DIM * STATE)
    unity = (jnp.ones((HEADS,), jnp.float32), jnp.zeros((HEADS, HEAD_DIM * STATE), jnp.float32))

    def advance(index, current):
        return shifted(decay[:, None] * current + flat_state, "ctx", 1)

    incoming = lax.fori_loop(
        0, lax.axis_size("ctx") - 1, advance, jnp.zeros((HEADS, HEAD_DIM * STATE), jnp.float32)
    )
    carried = incoming.reshape(HEADS, HEAD_DIM, STATE)
    final_output, layer_pull = jax.vjp(
        shard_layer,
        extended,
        gates,
        steps,
        taps,
        initial_offset,
        step_shift,
        damping_exponents,
        skip_values,
        gain_values,
        carried,
    )
    forward = shifted(final_output.astype(jnp.bfloat16)[None, None], "section", 1)
    grads = layer_pull(cotangent[0, 0].astype(jnp.float32))
    carry_grad = grads[9].reshape(HEADS, HEAD_DIM * STATE)
    outgoing = prefix((decay, carry_grad), "ctx", combine, unity)[1]
    outgoing_grad = outgoing.reshape(HEADS, HEAD_DIM, STATE)
    total_grad = jnp.sum(outgoing_grad * carried, axis=(1, 2)) * decay
    extra = state_pull((outgoing_grad, total_grad))
    ext_grad = grads[0] + extra[0]
    step_grad = grads[2] + extra[1]
    param_terms = (
        grads[3] + extra[2],
        grads[4] + extra[3],
        grads[5] + extra[4],
        grads[6] + extra[5],
        grads[7],
        grads[8],
    )
    returned = shifted(ext_grad[: CONV - 1], "ctx", -1)
    own_grad = ext_grad[CONV - 1 :]
    row_grad = jnp.concatenate(
        [own_grad[: count - (CONV - 1)], own_grad[count - (CONV - 1) :] + returned], 0
    )
    backward = shifted(
        (
            row_grad.astype(jnp.bfloat16)[None, None],
            grads[1].astype(jnp.bfloat16)[None, None],
            step_grad.astype(jnp.bfloat16)[None, None],
        ),
        "section",
        -1,
    )
    summed = lax.psum(
        (
            param_terms[0],
            param_terms[1],
            param_terms[2],
            param_terms[3],
            param_terms[4],
            param_terms[5],
        ),
        ("ctx", "dp"),
    )
    return (
        forward,
        backward[0],
        backward[1],
        backward[2],
        summed[0][None],
        summed[1][None],
        summed[2][None],
        summed[3][None],
        summed[4][None],
        summed[5][None],
    )


MESH = pl.DeviceIdType.MESH
F32 = jnp.float32
BF16 = jnp.bfloat16
INNER = HEADS * HEAD_DIM
REPS = HEADS // GROUPS
WIDE = REPS * HEAD_DIM
MIX = WIDE + 2 * STATE
HALF = GROUPS // 2
NN = ((1,), (0,))
NT = ((1,), (1,))
TN = ((0,), (0,))


def split(a):
    high = a.astype(BF16)
    return high, (a - high.astype(F32)).astype(BF16)


def dot(a, b, dims):
    return lax.dot_general(a, b, (dims, ((), ())), preferred_element_type=F32)


def dot3(a, b, dims):
    return dot(a[0], b[0], dims) + (dot(a[0], b[1], dims) + dot(a[1], b[0], dims))


def group_columns(g):
    return (
        pl.multiple_of(g * WIDE, 128),
        pl.multiple_of(INNER + g * STATE, 128),
        pl.multiple_of(INNER + (GROUPS + g) * STATE, 128),
    )


def pair_kernel(
    conv_in, gate_in, step_in, cot_in, w_ref, b_ref, sb_ref, dl_ref, sk_ref, ng_ref,
    nxt, gconv, ggate, gstep, packed,
    uin, steps, steprow, upad, zpad, mix, dsl, dtc, sigc, ratec, cumc, cumr, ddt, drate, small,
    stage_c, stage_o, stage_s, step_parts, partial, final, zeros,
    own_sem, xs_sem, xr_sem, st_sem, conv_sem, gate_sem, next_sem, dstep_sem,
    ps_sem, pr_sem, fin_sem, zero_sem,
):
    core = lax.axis_index("ctx")
    sec = lax.axis_index("section")
    dp = lax.axis_index("dp")
    nsec = lax.axis_size("section")
    ndp = lax.axis_size("dp")
    tok = conv_in.shape[2]
    seq = 2 * tok
    other = 1 - core

    def place(c, s, d):
        return {"ctx": c, "section": s, "dp": d}

    def remote(src, dst, send, recv, c, s, d):
        return pltpu.make_async_remote_copy(
            src_ref=src, dst_ref=dst, send_sem=send, recv_sem=recv,
            device_id=place(c, s, d), device_id_type=MESH,
        )

    after = lax.rem(sec + 1, nsec)
    before = lax.rem(sec + nsec - 1, nsec)
    barrier = pltpu.get_barrier_semaphore()

    def greet(c, s, d):
        pl.semaphore_signal(barrier, inc=1, device_id=place(c, s, d), device_id_type=MESH)

    greet(other, sec, dp)
    for c in range(2):
        greet(c, after, dp)
        greet(c, before, dp)
    for k in range(1, ndp):
        greet(core, sec, lax.rem(dp + k, ndp))

    def pieces(g):
        xc, bc, cc = group_columns(g)
        return (
            (conv_in.at[0, 0, :, pl.ds(xc, WIDE)], 0, WIDE),
            (conv_in.at[0, 0, :, pl.ds(bc, STATE)], WIDE, STATE),
            (conv_in.at[0, 0, :, pl.ds(cc, STATE)], WIDE + STATE, STATE),
            (gate_in.at[0, 0, :, pl.ds(xc, WIDE)], MIX, WIDE),
            (cot_in.at[0, 0, :, pl.ds(xc, WIDE)], MIX + WIDE, WIDE),
        )

    mine = pl.ds(pl.multiple_of(core * tok, tok), tok)
    theirs = pl.ds(pl.multiple_of(other * tok, tok), tok)
    own_step = pltpu.make_async_copy(step_in.at[0, 0], steps.at[core], st_sem.at[0])
    own_step.start()

    def fetch(j, _):
        for src, off, width in pieces(core * HALF + j):
            pltpu.make_async_copy(
                src, uin.at[j, mine, pl.ds(off, width)], own_sem.at[j]
            ).start()
        return 0

    lax.fori_loop(0, HALF, fetch, 0)
    zeros[...] = jnp.zeros_like(zeros)
    partial[dp] = jnp.zeros(partial.shape[1:], F32)
    upad[0:8, :] = jnp.zeros((8, MIX), F32)
    zpad[seq : seq + 8, :] = jnp.zeros((8, MIX), F32)
    for ref in (steprow, dtc, sigc, ratec, ddt, drate, small):
        ref[...] = jnp.zeros_like(ref)
    pl.semaphore_wait(barrier, 1 + 4 + (ndp - 1))
    step_copy = remote(
        step_in.at[0, 0], steps.at[core], st_sem.at[1], st_sem.at[2], other, sec, dp
    )
    step_copy.start()

    def exchange(j, _):
        for src, off, width in pieces(other * HALF + j):
            remote(
                src, uin.at[j, mine, pl.ds(off, width)], xs_sem.at[j], xr_sem.at[j], other, sec, dp
            ).start()
        return 0

    lax.fori_loop(0, HALF, exchange, 0)

    @pl.when(sec == 0)
    def _():
        pltpu.make_async_copy(zeros, nxt.at[0, 0], zero_sem.at[0]).start()

    @pl.when(sec == nsec - 1)
    def _():
        for part in range(5):
            pltpu.make_async_copy(
                zeros, gconv.at[0, 0, :, pl.ds(part * INNER, INNER)], zero_sem.at[1]
            ).start()
        pltpu.make_async_copy(zeros, ggate.at[0, 0], zero_sem.at[2]).start()

    own_step.wait()
    step_copy.wait()
    for c in range(2):
        steprow[0:HEADS, c * tok : (c + 1) * tok] = steps[c].astype(F32)
    raw = steprow[...].T[:, 0:HEADS] + sb_ref[...]
    delta = jnp.maximum(raw, 0.0) + jnp.log1p(jnp.exp(-jnp.abs(raw)))
    dtc[:, 0:HEADS] = delta
    sigc[:, 0:HEADS] = jax.nn.sigmoid(raw)
    ratec[:, 0:HEADS] = delta * (-jnp.exp(dl_ref[...]))
    rows2 = lax.broadcasted_iota(jnp.int32, (seq, seq), 0)
    cols2 = lax.broadcasted_iota(jnp.int32, (seq, seq), 1)
    ones_low = jnp.where(rows2 >= cols2, 1.0, 0.0).astype(BF16)
    rate = ratec[...]
    r_hi, r_rest = rate.astype(BF16), rate - rate.astype(BF16).astype(F32)
    r_mid, r_lo = split(r_rest)
    cumulative = dot(ones_low, r_hi, NN) + (dot(ones_low, r_mid, NN) + dot(ones_low, r_lo, NN))
    cumc[...] = cumulative
    cumr[...] = cumulative.T

    def group(j, _):
        g = core * HALF + j
        cols = group_columns(g)
        pltpu.make_async_copy(uin.at[j, mine], uin.at[j, mine], own_sem.at[j]).wait()
        remote(uin.at[j, mine], uin.at[j, theirs], xs_sem.at[j], xr_sem.at[j], other, sec, dp).wait()
        blocks = [(0, cols[0])]
        for base, col in ((WIDE, cols[1]), (WIDE + STATE, cols[2])):
            for part in range(STATE // 128):
                blocks.append((base + part * 128, pl.multiple_of(col + part * 128, 128)))

        for off, col in blocks:
            here = slice(off, off + 128)
            upad[8 : 8 + seq, here] = uin[j, :, here].astype(F32)
            z = b_ref[:, pl.ds(col, 128)]
            for k in range(CONV):
                z = z + w_ref[0, pl.ds(k, 1), pl.ds(col, 128)] * upad[5 + k : 5 + k + seq, here]
            s = jax.nn.sigmoid(z)
            mix[:, here] = z * s
            dsl[:, here] = s * (1.0 + z * (1.0 - s))

        lane = lax.broadcasted_iota(jnp.int32, (seq, 128), 1)
        lane1 = lax.broadcasted_iota(jnp.int32, (1, 128), 1)
        lane16 = lax.broadcasted_iota(jnp.int32, (1, HEADS), 1)
        row = lax.broadcasted_iota(jnp.int32, (seq, seq), 0)
        column = lax.broadcasted_iota(jnp.int32, (seq, seq), 1)
        first = lane < HEAD_DIM

        def pick(ref, h):
            return jnp.sum(jnp.where(lane == h, ref[...], 0.0), axis=1, keepdims=True)

        def pick1(ref, h):
            return jnp.sum(jnp.where(lane16 == h, ref[...], 0.0), axis=1, keepdims=True)

        x = mix[:, 0:WIDE]
        bmap = split(mix[:, WIDE : WIDE + STATE])
        cmap = split(mix[:, WIDE + STATE : MIX])
        h0 = g * REPS
        dt2 = jnp.where(first, pick(dtc, h0), pick(dtc, h0 + 1))
        skip2 = jnp.where(first[0:1], pick1(sk_ref, h0), pick1(sk_ref, h0 + 1))
        xs = x * dt2
        xs_p = split(xs)
        scores = dot3(cmap, bmap, NT)
        decay, mixed, ys = [], [], []
        for r in range(REPS):
            seg = pick(cumc, h0 + r) - cumr[pl.ds(h0 + r, 1), :]
            w = jnp.exp(jnp.where(row >= column, seg, -jnp.inf))
            a = scores * w
            a_p = split(a)
            decay.append(w)
            mixed.append((a, a_p))
            ys.append(dot3(a_p, xs_p, NN))
        y = jnp.where(first, ys[0], ys[1]) + skip2 * x
        gate = uin[j, :, MIX : MIX + WIDE].astype(F32)
        cot = uin[j, :, MIX + WIDE : MIX + 2 * WIDE].astype(F32)
        gain = ng_ref[:, pl.ds(cols[0], WIDE)]
        s = jax.nn.sigmoid(gate)
        act = gate * s
        gated = y * act
        scale = lax.rsqrt(jnp.mean(gated * gated, axis=1, keepdims=True) + 1e-05)
        normed = gated * scale
        stage_o[j, :, 0:WIDE] = (normed * gain).astype(BF16)
        dn = cot * gain
        dgated = scale * (dn - normed * jnp.mean(dn * normed, axis=1, keepdims=True))
        dy = dgated * act
        stage_o[j, :, WIDE : 2 * WIDE] = (dgated * y * (s * (1.0 + gate * (1.0 - s)))).astype(BF16)

        @pl.when(sec < nsec - 1)
        def _():
            for t in range(2):
                remote(
                    stage_o.at[j, pl.ds(t * tok, tok), pl.ds(0, WIDE)],
                    nxt.at[0, 0, :, pl.ds(cols[0], WIDE)],
                    next_sem.at[0], next_sem.at[1], t, sec + 1, dp,
                ).start()

        @pl.when(sec > 0)
        def _():
            for t in range(2):
                remote(
                    stage_o.at[j, pl.ds(t * tok, tok), pl.ds(WIDE, WIDE)],
                    ggate.at[0, 0, :, pl.ds(cols[0], WIDE)],
                    gate_sem.at[0], gate_sem.at[1], t, sec - 1, dp,
                ).start()

        partial[dp, j, 5:6, 0:WIDE] = jnp.sum(cot * normed, axis=0, keepdims=True)
        dyx = jnp.sum(dy * x, axis=0, keepdims=True)
        dscore = jnp.zeros((seq, seq), F32)
        dy_p = split(dy)
        das = []
        for r in range(REPS):
            own = first if r == 0 else jnp.logical_not(first)
            da = dot3(split(jnp.where(own, dy, 0.0)), xs_p, NT)
            das.append(da)
            dscore = dscore + da * decay[r]
        ds_p = split(dscore)

        def conv_back(off, width, start):
            for part in range(width // 128):
                here = slice(off + part * 128, off + part * 128 + 128)
                col = pl.multiple_of(start + part * 128, 128)
                dz = zpad[0:seq, here]
                du = jnp.zeros((seq, 128), F32)
                for k in range(CONV):
                    du = du + w_ref[0, pl.ds(k, 1), pl.ds(col, 128)] * zpad[3 - k : 3 - k + seq, here]
                    partial[dp, j, pl.ds(k, 1), here] = jnp.sum(
                        dz * upad[5 + k : 5 + k + seq, here], axis=0, keepdims=True
                    )
                partial[dp, j, pl.ds(4, 1), here] = jnp.sum(dz, axis=0, keepdims=True)
                stage_c[j, :, here] = du.astype(BF16)

            @pl.when(sec > 0)
            def _():
                for t in range(2):
                    remote(
                        stage_c.at[j, pl.ds(t * tok, tok), pl.ds(off, width)],
                        gconv.at[0, 0, :, pl.ds(start, width)],
                        conv_sem.at[0], conv_sem.at[1], t, sec - 1, dp,
                    ).start()

        zpad[0:seq, WIDE + STATE : MIX] = dot3(ds_p, bmap, NN) * dsl[:, WIDE + STATE : MIX]
        conv_back(WIDE + STATE, STATE, cols[2])
        zpad[0:seq, WIDE : WIDE + STATE] = dot3(ds_p, cmap, TN) * dsl[:, WIDE : WIDE + STATE]
        conv_back(WIDE, STATE, cols[1])
        dxs = jnp.where(first, dot3(mixed[0][1], dy_p, TN), dot3(mixed[1][1], dy_p, TN))
        zpad[0:seq, 0:WIDE] = (skip2 * dy + dxs * dt2) * dsl[:, 0:WIDE]
        conv_back(0, WIDE, cols[0])
        upper = jnp.where(row <= column, 1.0, 0.0).astype(BF16)
        dxx = dxs * x
        for r in range(REPS):
            own = first if r == 0 else jnp.logical_not(first)
            p = split(das[r] * mixed[r][0])
            later = dot(upper, p[0], NN) + dot(upper, p[1], NN)
            dr = jnp.sum(jnp.where(row > column, later, 0.0), axis=1, keepdims=True)
            drate[...] += jnp.where(lane == h0 + r, dr, 0.0)
            total = jnp.sum(jnp.where(own[0:1], dyx, 0.0), axis=1, keepdims=True)
            small[2:3, :] += jnp.where(lane1 == h0 + r, total, 0.0)
            dd = jnp.sum(jnp.where(own, dxx, 0.0), axis=1, keepdims=True)
            ddt[...] += jnp.where(lane == h0 + r, dd, 0.0)

        for k in range(1, ndp):
            to = lax.rem(dp + k, ndp)
            remote(
                partial.at[dp, j], partial.at[dp, j], ps_sem.at[to], pr_sem.at[dp], core, sec, to
            ).start()
        return 0

    lax.fori_loop(0, HALF, group, 0)

    damp = jnp.exp(dl_ref[...])
    dr16 = drate[:, 0:HEADS]
    dstep = (ddt[:, 0:HEADS] - dr16 * damp) * sigc[:, 0:HEADS]
    small[0:1, 0:HEADS] = jnp.sum(dstep, axis=0, keepdims=True)
    small[1:2, 0:HEADS] = jnp.sum(dr16 * ratec[:, 0:HEADS], axis=0, keepdims=True)
    drate[:, 0:HEADS] = dstep
    turned = drate[...].T
    for t in range(2):
        stage_s[t] = turned[0:HEADS, t * tok : (t + 1) * tok].astype(BF16)

    @pl.when(sec > 0)
    def _():
        for t in range(2):
            remote(
                stage_s.at[t], step_parts.at[core],
                dstep_sem.at[2], dstep_sem.at[core], t, sec - 1, dp,
            ).start()

    partial[dp, HALF, :, 0:128] = small[...]
    for k in range(1, ndp):
        to = lax.rem(dp + k, ndp)
        remote(
            partial.at[dp, HALF], partial.at[dp, HALF], ps_sem.at[to], pr_sem.at[dp], core, sec, to
        ).start()
    for k in range(1, ndp):
        to = lax.rem(dp + k, ndp)
        remote(partial.at[dp], partial.at[to], ps_sem.at[to], pr_sem.at[to], core, sec, to).wait()
    total = partial[0]
    for k in range(1, ndp):
        total = total + partial[k]
    final[core] = total
    halves = remote(final.at[core], final.at[core], fin_sem.at[0], fin_sem.at[1], other, sec, dp)
    halves.start()
    remote(final.at[core], final.at[other], fin_sem.at[0], fin_sem.at[1], other, sec, dp).wait()
    packed[...] = final[...]

    @pl.when(sec == 0)
    def _():
        pltpu.make_async_copy(zeros, nxt.at[0, 0], zero_sem.at[0]).wait()

    @pl.when(sec > 0)
    def _():
        low = sec - 1
        remote(stage_c, stage_c, conv_sem.at[0], conv_sem.at[1], core, low, dp).wait_send()
        half_o = stage_o.at[:, :, pl.ds(0, WIDE)]
        remote(half_o, half_o, gate_sem.at[0], gate_sem.at[1], core, low, dp).wait_send()
        remote(stage_s, stage_s, dstep_sem.at[2], dstep_sem.at[0], core, low, dp).wait_send()
        remote(
            nxt.at[0, 0], nxt.at[0, 0], next_sem.at[0], next_sem.at[1], core, low, dp
        ).wait_recv()

    @pl.when(sec == nsec - 1)
    def _():
        whole = gconv.at[0, 0]
        pltpu.make_async_copy(whole, whole, zero_sem.at[1]).wait()
        pltpu.make_async_copy(zeros, ggate.at[0, 0], zero_sem.at[2]).wait()
        gstep[...] = jnp.zeros_like(gstep)

    @pl.when(sec < nsec - 1)
    def _():
        high = sec + 1
        half_o = stage_o.at[:, :, pl.ds(0, WIDE)]
        remote(half_o, half_o, next_sem.at[0], next_sem.at[1], core, high, dp).wait_send()
        for c in range(2):
            part = step_parts.at[c]
            remote(part, part, dstep_sem.at[2], dstep_sem.at[c], core, high, dp).wait_recv()
        gstep[0, 0] = (step_parts[0].astype(F32) + step_parts[1].astype(F32)).astype(BF16)
        whole = ggate.at[0, 0]
        remote(whole, whole, gate_sem.at[0], gate_sem.at[1], core, high, dp).wait_recv()
        whole = gconv.at[0, 0]
        remote(whole, whole, conv_sem.at[0], conv_sem.at[1], core, high, dp).wait_recv()


def finish_kernel(
    nxt_in, gconv_in, ggate_in, gstep_in, packed,
    nxt, gconv, ggate, gstep, gtap, gcb, gsb, gdl, gsk, gng,
    held, in_sem, out_sem,
):
    routes = [(nxt_in.at[0, 0], nxt.at[0, 0]), (ggate_in.at[0, 0], ggate.at[0, 0])]
    for part in range(5):
        cut = pl.ds(part * INNER, INNER)
        routes.append((gconv_in.at[0, 0, :, cut], gconv.at[0, 0, :, cut]))
    arrive = [pltpu.make_async_copy(r[0], held.at[i], in_sem.at[i]) for i, r in enumerate(routes)]
    leave = [pltpu.make_async_copy(held.at[i], r[1], out_sem.at[i]) for i, r in enumerate(routes)]
    for copy in arrive:
        copy.start()
    gstep[...] = gstep_in[...]
    for g in range(GROUPS):
        c, j = g // HALF, g % HALF
        gng[0:1, g * WIDE : (g + 1) * WIDE] = packed[c, j, 5:6, 0:WIDE]
        for off, width, col in (
            (0, WIDE, g * WIDE),
            (WIDE, STATE, INNER + g * STATE),
            (WIDE + STATE, STATE, INNER + (GROUPS + g) * STATE),
        ):
            gtap[0, :, col : col + width] = packed[c, j, 0:CONV, off : off + width]
            gcb[0:1, col : col + width] = packed[c, j, CONV : CONV + 1, off : off + width]
    for at, ref in enumerate((gsb, gdl, gsk)):
        ref[...] = packed[0, HALF, at : at + 1, 0:HEADS] + packed[1, HALF, at : at + 1, 0:HEADS]
    for into, out in zip(arrive, leave):
        into.wait()
        out.start()
    for out in leave:
        out.wait()


def paired(
    conv_input, gate_input, step_input, cotangent, conv_weight,
    conv_bias, step_bias, decay_log, skip_gain, norm_gain,
):
    tok = conv_input.shape[2]
    seq = 2 * tok
    ndp = lax.axis_size("dp")
    hbm = pl.BlockSpec(memory_space=pl.ANY)
    vmem = pl.BlockSpec(memory_space=pltpu.VMEM)
    like = lambda a, kind: jax.ShapeDtypeStruct(a.shape, kind)
    scratch = [
        pltpu.VMEM((HALF, seq, MIX + 2 * WIDE), BF16),
        pltpu.VMEM((2, HEADS, tok), BF16),
        pltpu.VMEM((128, seq), F32),
        pltpu.VMEM((seq + 8, MIX), F32),
        pltpu.VMEM((seq + 8, MIX), F32),
        pltpu.VMEM((seq, MIX), F32),
        pltpu.VMEM((seq, MIX), F32),
        pltpu.VMEM((seq, 128), F32),
        pltpu.VMEM((seq, 128), F32),
        pltpu.VMEM((seq, 128), F32),
        pltpu.VMEM((seq, 128), F32),
        pltpu.VMEM((128, seq), F32),
        pltpu.VMEM((seq, 128), F32),
        pltpu.VMEM((seq, 128), F32),
        pltpu.VMEM((8, 128), F32),
        pltpu.VMEM((HALF, seq, MIX), BF16),
        pltpu.VMEM((HALF, seq, 2 * WIDE), BF16),
        pltpu.VMEM((2, HEADS, tok), BF16),
        pltpu.VMEM((2, HEADS, tok), BF16),
        pltpu.VMEM((ndp, HALF + 1, 8, MIX), F32),
        pltpu.VMEM((2, HALF + 1, 8, MIX), F32),
        pltpu.VMEM((tok, INNER), BF16),
        pltpu.SemaphoreType.DMA((HALF,)),
        pltpu.SemaphoreType.DMA((HALF,)),
        pltpu.SemaphoreType.DMA((HALF,)),
        pltpu.SemaphoreType.DMA((3,)),
        pltpu.SemaphoreType.DMA((2,)),
        pltpu.SemaphoreType.DMA((2,)),
        pltpu.SemaphoreType.DMA((2,)),
        pltpu.SemaphoreType.DMA((3,)),
        pltpu.SemaphoreType.DMA((ndp,)),
        pltpu.SemaphoreType.DMA((ndp,)),
        pltpu.SemaphoreType.DMA((2,)),
        pltpu.SemaphoreType.DMA((3,)),
    ]
    turned = jnp.swapaxes(step_input, 2, 3)
    sent = pl.pallas_call(
        pair_kernel,
        name="mixer_tick",
        in_specs=[hbm] * 4 + [vmem] * 6,
        out_specs=[hbm] * 3 + [vmem] * 2,
        out_shape=[
            like(gate_input, BF16),
            like(conv_input, BF16),
            like(gate_input, BF16),
            like(turned, BF16),
            jax.ShapeDtypeStruct((2, HALF + 1, 8, MIX), F32),
        ],
        scratch_shapes=scratch,
        compiler_params=pltpu.CompilerParams(collective_id=0, has_side_effects=True),
    )(
        conv_input, gate_input, turned, cotangent, conv_weight,
        conv_bias, step_bias, decay_log, skip_gain, norm_gain,
    )
    done = pl.pallas_call(
        finish_kernel,
        name="mixer_finish",
        in_specs=[hbm] * 3 + [vmem] * 2,
        out_specs=[hbm] * 3 + [vmem] * 7,
        out_shape=[
            like(gate_input, BF16),
            like(conv_input, BF16),
            like(gate_input, BF16),
            like(turned, BF16),
            like(conv_weight, F32),
            like(conv_bias, F32),
            like(step_bias, F32),
            like(decay_log, F32),
            like(skip_gain, F32),
            like(norm_gain, F32),
        ],
        scratch_shapes=[
            pltpu.VMEM((7, tok, INNER), BF16),
            pltpu.SemaphoreType.DMA((7,)),
            pltpu.SemaphoreType.DMA((7,)),
        ],
    )(*sent)
    return tuple(done[:3]) + (jnp.swapaxes(done[3], 2, 3),) + tuple(done[4:])


def solution(mesh):
    in_specs = (
        P("section", "dp", "ctx", None),
        P("section", "dp", "ctx", None),
        P("section", "dp", "ctx", None),
        P("section", "dp", "ctx", None),
        P("section", None, None),
        P("section", None),
        P("section", None),
        P("section", None),
        P("section", None),
        P("section", None),
    )
    out_specs = (
        P("section", "dp", "ctx", None),
        P("section", "dp", "ctx", None),
        P("section", "dp", "ctx", None),
        P("section", "dp", "ctx", None),
        P("section", None, None),
        P("section", None),
        P("section", None),
        P("section", None),
        P("section", None),
        P("section", None),
    )
    body = paired if mesh.shape["ctx"] == 2 else shards
    return jax.shard_map(body, mesh=mesh, in_specs=in_specs, out_specs=out_specs, check_vma=False)
```

```python
import functools
import jax
import jax.numpy as jnp
from jax import lax
from jax.experimental import pallas as pl
from jax.experimental.pallas import tpu as pltpu
from jax.sharding import PartitionSpec as P

HEADS = 16
HEAD_DIM = 64
STATE = 256
GROUPS = 8
CONV = 4


HIGH_BOUND = lax.Precision.HIGHEST


def shifted(block, axis, distance):
    devices = range(lax.axis_size(axis))
    route = [(i - distance, i) for i in devices if i - distance in devices]
    return lax.ppermute(block, axis, route)


def prefix(part, axis, combine, identity):
    count = lax.axis_size(axis)
    place = lax.axis_index(axis)
    ahead = count - 1 - place
    gathered = jax.tree.map(lambda a: lax.all_gather(a, axis), part)
    state = jax.tree.map(lambda a, e: jnp.zeros_like(a) + jnp.asarray(e, a.dtype), part, identity)

    def one(turn, state):
        source = count - 1 - turn
        return combine(
            state, jax.tree.map(lambda a: lax.dynamic_index_in_dim(a, source, 0, False), gathered)
        )

    return lax.fori_loop(0, ahead, one, state)


def conv_mix(extended, taps, initial_offset):
    rows = extended.shape[0] - (CONV - 1)
    total = initial_offset[None, :]
    for tap in range(CONV):
        total = total + taps[tap][None, :] * extended[tap : tap + rows]
    return jax.nn.silu(total)


def split_mix(mixed, steps, step_shift, damping_exponents):
    rows = mixed.shape[0]
    inner = HEADS * HEAD_DIM
    payload_lines = mixed[:, :inner].reshape(rows, GROUPS, HEADS // GROUPS, HEAD_DIM)
    in_maps = mixed[:, inner : inner + GROUPS * STATE].reshape(rows, GROUPS, STATE)
    out_maps = mixed[:, inner + GROUPS * STATE :].reshape(rows, GROUPS, STATE)
    delta = jax.nn.softplus(steps + step_shift[None, :])
    cumulative = jnp.cumsum(delta * (-jnp.exp(damping_exponents))[None, :], axis=0)
    return (payload_lines, in_maps, out_maps, delta, cumulative)


def fragment_condition(extended, steps, taps, initial_offset, step_shift, damping_exponents):
    payload_lines, in_maps, out_maps, delta, cumulative = split_mix(
        conv_mix(extended, taps, initial_offset), steps, step_shift, damping_exponents
    )
    rows = payload_lines.shape[0]
    total = cumulative[-1]
    weight = (jnp.exp(total[None, :] - cumulative) * delta).reshape(rows, GROUPS, HEADS // GROUPS)
    state = jnp.einsum(
        "tgrp,tgn->grpn", payload_lines * weight[..., None], in_maps, precision=HIGH_BOUND
    )
    return (state.reshape(HEADS, HEAD_DIM, STATE), total)


def shard_layer(
    extended,
    gates,
    steps,
    taps,
    initial_offset,
    step_shift,
    damping_exponents,
    skip_values,
    gain_values,
    carried,
):
    payload_lines, in_maps, out_maps, delta, cumulative = split_mix(
        conv_mix(extended, taps, initial_offset), steps, step_shift, damping_exponents
    )
    rows = payload_lines.shape[0]
    reps = HEADS // GROUPS
    lower = (jnp.arange(rows)[:, None] >= jnp.arange(rows)[None, :])[None]
    seg = cumulative.T[:, :, None] - cumulative.T[:, None, :]
    weight = jnp.exp(jnp.where(lower, seg, -jnp.inf)).reshape(GROUPS, reps, rows, rows)
    intersection_maps = jnp.einsum("tgn,sgn->gts", out_maps, in_maps, precision=HIGH_BOUND)
    score_matrix = weight * intersection_maps[:, None]
    scaled_values = payload_lines * delta.reshape(rows, GROUPS, reps)[..., None]
    final_output = jnp.einsum("jzlh,hjzc->ljzc", score_matrix, scaled_values, precision=HIGH_BOUND)
    incoming = jnp.einsum(
        "tgn,grpn->tgrp",
        out_maps,
        carried.reshape(GROUPS, reps, HEAD_DIM, STATE),
        precision=HIGH_BOUND,
    )
    final_output = (
        final_output + incoming * jnp.exp(cumulative).reshape(rows, GROUPS, reps)[..., None]
    )
    final_output = (
        final_output + skip_values.reshape(GROUPS, reps)[None, :, :, None] * payload_lines
    )
    gated = final_output.reshape(rows, GROUPS, -1) * jax.nn.silu(gates).reshape(rows, GROUPS, -1)
    normed = gated * lax.rsqrt(jnp.mean(gated * gated, axis=-1, keepdims=True) + 1e-05)
    return normed.reshape(rows, -1) * gain_values[None, :]


def combine(earlier, later):
    return (earlier[0] * later[0], later[0][:, None] * earlier[1] + later[1])


def shards(
    conv_input,
    gate_input,
    step_input,
    cotangent,
    conv_weight,
    conv_bias,
    step_bias,
    decay_log,
    skip_gain,
    norm_gain,
):
    local_rows = conv_input[0, 0]
    count = local_rows.shape[0]
    taps, initial_offset = (conv_weight[0], conv_bias[0])
    step_shift, damping_exponents = (step_bias[0], decay_log[0])
    skip_values, gain_values = (skip_gain[0], norm_gain[0])
    previous = shifted(local_rows[count - (CONV - 1) :], "ctx", 1)
    extended = jnp.concatenate([previous, local_rows], 0).astype(jnp.float32)
    gates = gate_input[0, 0].astype(jnp.float32)
    steps = step_input[0, 0].astype(jnp.float32)
    (state, total), state_pull = jax.vjp(
        fragment_condition, extended, steps, taps, initial_offset, step_shift, damping_exponents
    )
    decay = jnp.exp(total)
    flat_state = state.reshape(HEADS, HEAD_DIM * STATE)
    unity = (jnp.ones((HEADS,), jnp.float32), jnp.zeros((HEADS, HEAD_DIM * STATE), jnp.float32))

    def advance(index, current):
        return shifted(decay[:, None] * current + flat_state, "ctx", 1)

    incoming = lax.fori_loop(
        0, lax.axis_size("ctx") - 1, advance, jnp.zeros((HEADS, HEAD_DIM * STATE), jnp.float32)
    )
    carried = incoming.reshape(HEADS, HEAD_DIM, STATE)
    final_output, layer_pull = jax.vjp(
        shard_layer,
        extended,
        gates,
        steps,
        taps,
        initial_offset,
        step_shift,
        damping_exponents,
        skip_values,
        gain_values,
        carried,
    )
    forward = shifted(final_output.astype(jnp.bfloat16)[None, None], "section", 1)
    grads = layer_pull(cotangent[0, 0].astype(jnp.float32))
    carry_grad = grads[9].reshape(HEADS, HEAD_DIM * STATE)
    outgoing = prefix((decay, carry_grad), "ctx", combine, unity)[1]
    outgoing_grad = outgoing.reshape(HEADS, HEAD_DIM, STATE)
    total_grad = jnp.sum(outgoing_grad * carried, axis=(1, 2)) * decay
    extra = state_pull((outgoing_grad, total_grad))
    ext_grad = grads[0] + extra[0]
    step_grad = grads[2] + extra[1]
    param_terms = (
        grads[3] + extra[2],
        grads[4] + extra[3],
        grads[5] + extra[4],
        grads[6] + extra[5],
        grads[7],
        grads[8],
    )
    returned = shifted(ext_grad[: CONV - 1], "ctx", -1)
    own_grad = ext_grad[CONV - 1 :]
    row_grad = jnp.concatenate(
        [own_grad[: count - (CONV - 1)], own_grad[count - (CONV - 1) :] + returned], 0
    )
    backward = shifted(
        (
            row_grad.astype(jnp.bfloat16)[None, None],
            grads[1].astype(jnp.bfloat16)[None, None],
            step_grad.astype(jnp.bfloat16)[None, None],
        ),
        "section",
        -1,
    )
    summed = lax.psum(
        (
            param_terms[0],
            param_terms[1],
            param_terms[2],
            param_terms[3],
            param_terms[4],
            param_terms[5],
        ),
        ("ctx", "dp"),
    )
    return (
        forward,
        backward[0],
        backward[1],
        backward[2],
        summed[0][None],
        summed[1][None],
        summed[2][None],
        summed[3][None],
        summed[4][None],
        summed[5][None],
    )


MESH = pl.DeviceIdType.MESH
F32 = jnp.float32
BF16 = jnp.bfloat16
INNER = HEADS * HEAD_DIM
REPS = HEADS // GROUPS
WIDE = REPS * HEAD_DIM
MIX = WIDE + 2 * STATE
HALF = GROUPS // 2
NN = ((1,), (0,))
NT = ((1,), (1,))
TN = ((0,), (0,))


def split(a):
    high = a.astype(BF16)
    return high, (a - high.astype(F32)).astype(BF16)


def dot(a, b, dims):
    return lax.dot_general(a, b, (dims, ((), ())), preferred_element_type=F32)


def dot3(a, b, dims):
    return dot(a[0], b[0], dims) + (dot(a[0], b[1], dims) + dot(a[1], b[0], dims))


def group_columns(g):
    return (
        pl.multiple_of(g * WIDE, 128),
        pl.multiple_of(INNER + g * STATE, 128),
        pl.multiple_of(INNER + (GROUPS + g) * STATE, 128),
    )


def pair_kernel(
    conv_in, gate_in, step_in, cot_in, w_ref, b_ref, sb_ref, dl_ref, sk_ref, ng_ref,
    nxt, gconv, ggate, gstep, packed,
    uin, steps, steprow, upad, zpad, mix, dsl, dtc, sigc, ratec, cumc, cumr, ddt, drate, small,
    stage_c, stage_o, stage_s, step_parts, partial, final, zeros, relay,
    own_sem, xs_sem, xr_sem, st_sem, conv_sem, gate_sem, next_sem, dstep_sem,
    ps_sem, pr_sem, fin_sem, zero_sem, via_sem, relay_sem,
):
    core = lax.axis_index("ctx")
    sec = lax.axis_index("section")
    dp = lax.axis_index("dp")
    nsec = lax.axis_size("section")
    ndp = lax.axis_size("dp")
    tok = conv_in.shape[2]
    seq = 2 * tok
    other = 1 - core

    def place(c, s, d):
        return {"ctx": c, "section": s, "dp": d}

    def remote(src, dst, send, recv, c, s, d):
        return pltpu.make_async_remote_copy(
            src_ref=src, dst_ref=dst, send_sem=send, recv_sem=recv,
            device_id=place(c, s, d), device_id_type=MESH,
        )

    after = lax.rem(sec + 1, nsec)
    before = lax.rem(sec + nsec - 1, nsec)
    barrier = pltpu.get_barrier_semaphore()

    def greet(c, s, d):
        pl.semaphore_signal(barrier, inc=1, device_id=place(c, s, d), device_id_type=MESH)

    greet(other, sec, dp)
    for c in range(2):
        greet(c, after, dp)
        greet(c, before, dp)
        greet(c, lax.rem(sec + 2, nsec), dp)
    for k in range(1, ndp):
        greet(core, sec, lax.rem(dp + k, ndp))

    def pieces(g):
        xc, bc, cc = group_columns(g)
        return (
            (conv_in.at[0, 0, :, pl.ds(xc, WIDE)], 0, WIDE),
            (conv_in.at[0, 0, :, pl.ds(bc, STATE)], WIDE, STATE),
            (conv_in.at[0, 0, :, pl.ds(cc, STATE)], WIDE + STATE, STATE),
            (gate_in.at[0, 0, :, pl.ds(xc, WIDE)], MIX, WIDE),
            (cot_in.at[0, 0, :, pl.ds(xc, WIDE)], MIX + WIDE, WIDE),
        )

    mine = pl.ds(pl.multiple_of(core * tok, tok), tok)
    theirs = pl.ds(pl.multiple_of(other * tok, tok), tok)
    own_step = pltpu.make_async_copy(step_in.at[0, 0], steps.at[core], st_sem.at[0])
    own_step.start()

    def fetch(j, _):
        for src, off, width in pieces(core * HALF + j):
            pltpu.make_async_copy(
                src, uin.at[j, mine, pl.ds(off, width)], own_sem.at[j]
            ).start()
        return 0

    lax.fori_loop(0, HALF, fetch, 0)
    zeros[...] = jnp.zeros_like(zeros)
    partial[dp] = jnp.zeros(partial.shape[1:], F32)
    upad[0:8, :] = jnp.zeros((8, MIX), F32)
    zpad[seq : seq + 8, :] = jnp.zeros((8, MIX), F32)
    for ref in (steprow, dtc, sigc, ratec, ddt, drate, small):
        ref[...] = jnp.zeros_like(ref)
    pl.semaphore_wait(barrier, 1 + 6 + (ndp - 1))
    step_copy = remote(
        step_in.at[0, 0], steps.at[core], st_sem.at[1], st_sem.at[2], other, sec, dp
    )
    step_copy.start()

    def exchange(j, _):
        for src, off, width in pieces(other * HALF + j):
            remote(
                src, uin.at[j, mine, pl.ds(off, width)], xs_sem.at[j], xr_sem.at[j], other, sec, dp
            ).start()
        return 0

    lax.fori_loop(0, HALF, exchange, 0)

    @pl.when(sec == 0)
    def _():
        pltpu.make_async_copy(zeros, nxt.at[0, 0], zero_sem.at[0]).start()

    @pl.when(sec == nsec - 1)
    def _():
        for part in range(5):
            pltpu.make_async_copy(
                zeros, gconv.at[0, 0, :, pl.ds(part * INNER, INNER)], zero_sem.at[1]
            ).start()
        pltpu.make_async_copy(zeros, ggate.at[0, 0], zero_sem.at[2]).start()

    own_step.wait()
    step_copy.wait()
    for c in range(2):
        steprow[0:HEADS, c * tok : (c + 1) * tok] = steps[c].astype(F32)
    raw = steprow[...].T[:, 0:HEADS] + sb_ref[...]
    delta = jnp.maximum(raw, 0.0) + jnp.log1p(jnp.exp(-jnp.abs(raw)))
    dtc[:, 0:HEADS] = delta
    sigc[:, 0:HEADS] = jax.nn.sigmoid(raw)
    ratec[:, 0:HEADS] = delta * (-jnp.exp(dl_ref[...]))
    rows2 = lax.broadcasted_iota(jnp.int32, (seq, seq), 0)
    cols2 = lax.broadcasted_iota(jnp.int32, (seq, seq), 1)
    ones_low = jnp.where(rows2 >= cols2, 1.0, 0.0).astype(BF16)
    rate = ratec[...]
    r_hi, r_rest = rate.astype(BF16), rate - rate.astype(BF16).astype(F32)
    r_mid, r_lo = split(r_rest)
    cumulative = dot(ones_low, r_hi, NN) + (dot(ones_low, r_mid, NN) + dot(ones_low, r_lo, NN))
    cumc[...] = cumulative
    cumr[...] = cumulative.T

    def group(j, _):
        g = core * HALF + j
        cols = group_columns(g)
        pltpu.make_async_copy(uin.at[j, mine], uin.at[j, mine], own_sem.at[j]).wait()
        remote(uin.at[j, mine], uin.at[j, theirs], xs_sem.at[j], xr_sem.at[j], other, sec, dp).wait()
        blocks = [(0, cols[0])]
        for base, col in ((WIDE, cols[1]), (WIDE + STATE, cols[2])):
            for part in range(STATE // 128):
                blocks.append((base + part * 128, pl.multiple_of(col + part * 128, 128)))

        for off, col in blocks:
            here = slice(off, off + 128)
            upad[8 : 8 + seq, here] = uin[j, :, here].astype(F32)
            z = b_ref[:, pl.ds(col, 128)]
            for k in range(CONV):
                z = z + w_ref[0, pl.ds(k, 1), pl.ds(col, 128)] * upad[5 + k : 5 + k + seq, here]
            s = jax.nn.sigmoid(z)
            mix[:, here] = z * s
            dsl[:, here] = s * (1.0 + z * (1.0 - s))

        lane = lax.broadcasted_iota(jnp.int32, (seq, 128), 1)
        lane1 = lax.broadcasted_iota(jnp.int32, (1, 128), 1)
        lane16 = lax.broadcasted_iota(jnp.int32, (1, HEADS), 1)
        row = lax.broadcasted_iota(jnp.int32, (seq, seq), 0)
        column = lax.broadcasted_iota(jnp.int32, (seq, seq), 1)
        first = lane < HEAD_DIM

        def pick(ref, h):
            return jnp.sum(jnp.where(lane == h, ref[...], 0.0), axis=1, keepdims=True)

        def pick1(ref, h):
            return jnp.sum(jnp.where(lane16 == h, ref[...], 0.0), axis=1, keepdims=True)

        x = mix[:, 0:WIDE]
        bmap = split(mix[:, WIDE : WIDE + STATE])
        cmap = split(mix[:, WIDE + STATE : MIX])
        h0 = g * REPS
        dt2 = jnp.where(first, pick(dtc, h0), pick(dtc, h0 + 1))
        skip2 = jnp.where(first[0:1], pick1(sk_ref, h0), pick1(sk_ref, h0 + 1))
        xs = x * dt2
        xs_p = split(xs)
        scores = dot3(cmap, bmap, NT)
        decay, mixed, ys = [], [], []
        for r in range(REPS):
            seg = pick(cumc, h0 + r) - cumr[pl.ds(h0 + r, 1), :]
            w = jnp.exp(jnp.where(row >= column, seg, -jnp.inf))
            a = scores * w
            a_p = split(a)
            decay.append(w)
            mixed.append((a, a_p))
            ys.append(dot3(a_p, xs_p, NN))
        y = jnp.where(first, ys[0], ys[1]) + skip2 * x
        gate = uin[j, :, MIX : MIX + WIDE].astype(F32)
        cot = uin[j, :, MIX + WIDE : MIX + 2 * WIDE].astype(F32)
        gain = ng_ref[:, pl.ds(cols[0], WIDE)]
        s = jax.nn.sigmoid(gate)
        act = gate * s
        gated = y * act
        scale = lax.rsqrt(jnp.mean(gated * gated, axis=1, keepdims=True) + 1e-05)
        normed = gated * scale
        stage_o[j, :, 0:WIDE] = (normed * gain).astype(BF16)
        dn = cot * gain
        dgated = scale * (dn - normed * jnp.mean(dn * normed, axis=1, keepdims=True))
        dy = dgated * act
        stage_o[j, :, WIDE : 2 * WIDE] = (dgated * y * (s * (1.0 + gate * (1.0 - s)))).astype(BF16)

        odd = lax.rem(j, 2) == 1

        def send_half(base, t, dst, done, landed, s):
            remote(
                stage_o.at[j, pl.ds(t * tok, tok), pl.ds(base, WIDE)], dst, done, landed, t, s, dp
            ).start()

        @pl.when(jnp.logical_and(sec < nsec - 1, jnp.logical_not(jnp.logical_and(sec == 1, odd))))
        def _():
            for t in range(2):
                send_half(
                    0, t, nxt.at[0, 0, :, pl.ds(cols[0], WIDE)],
                    next_sem.at[0], next_sem.at[1], sec + 1,
                )

        @pl.when(jnp.logical_and(sec == 1, odd))
        def _():
            slot = core * (HALF // 2) + j // 2
            for t in range(2):
                send_half(0, t, relay.at[slot], next_sem.at[0], relay_sem.at[slot], 3)

        @pl.when(jnp.logical_or(sec == 1, sec == 3))
        def _():
            for t in range(2):
                send_half(
                    WIDE, t, ggate.at[0, 0, :, pl.ds(cols[0], WIDE)],
                    gate_sem.at[0], gate_sem.at[1], sec - 1,
                )

        @pl.when(sec == 2)
        def _():
            slot = core * HALF + j
            for t in range(2):
                send_half(WIDE, t, relay.at[slot], gate_sem.at[0], relay_sem.at[slot], 0)

        partial[dp, j, 5:6, 0:WIDE] = jnp.sum(cot * normed, axis=0, keepdims=True)
        dyx = jnp.sum(dy * x, axis=0, keepdims=True)
        dscore = jnp.zeros((seq, seq), F32)
        dy_p = split(dy)
        das = []
        for r in range(REPS):
            own = first if r == 0 else jnp.logical_not(first)
            da = dot3(split(jnp.where(own, dy, 0.0)), xs_p, NT)
            das.append(da)
            dscore = dscore + da * decay[r]
        ds_p = split(dscore)

        def conv_back(off, width, start):
            for part in range(width // 128):
                here = slice(off + part * 128, off + part * 128 + 128)
                col = pl.multiple_of(start + part * 128, 128)
                dz = zpad[0:seq, here]
                du = jnp.zeros((seq, 128), F32)
                for k in range(CONV):
                    du = du + w_ref[0, pl.ds(k, 1), pl.ds(col, 128)] * zpad[3 - k : 3 - k + seq, here]
                    partial[dp, j, pl.ds(k, 1), here] = jnp.sum(
                        dz * upad[5 + k : 5 + k + seq, here], axis=0, keepdims=True
                    )
                partial[dp, j, pl.ds(4, 1), here] = jnp.sum(dz, axis=0, keepdims=True)
                stage_c[j, :, here] = du.astype(BF16)

            @pl.when(sec > 0)
            def _():
                for t in range(2):
                    remote(
                        stage_c.at[j, pl.ds(t * tok, tok), pl.ds(off, width)],
                        gconv.at[0, 0, :, pl.ds(start, width)],
                        conv_sem.at[0], conv_sem.at[1], t, sec - 1, dp,
                    ).start()

        zpad[0:seq, WIDE + STATE : MIX] = dot3(ds_p, bmap, NN) * dsl[:, WIDE + STATE : MIX]
        conv_back(WIDE + STATE, STATE, cols[2])
        zpad[0:seq, WIDE : WIDE + STATE] = dot3(ds_p, cmap, TN) * dsl[:, WIDE : WIDE + STATE]
        conv_back(WIDE, STATE, cols[1])
        dxs = jnp.where(first, dot3(mixed[0][1], dy_p, TN), dot3(mixed[1][1], dy_p, TN))
        zpad[0:seq, 0:WIDE] = (skip2 * dy + dxs * dt2) * dsl[:, 0:WIDE]
        conv_back(0, WIDE, cols[0])
        upper = jnp.where(row <= column, 1.0, 0.0).astype(BF16)
        dxx = dxs * x
        for r in range(REPS):
            own = first if r == 0 else jnp.logical_not(first)
            p = split(das[r] * mixed[r][0])
            later = dot(upper, p[0], NN) + dot(upper, p[1], NN)
            dr = jnp.sum(jnp.where(row > column, later, 0.0), axis=1, keepdims=True)
            drate[...] += jnp.where(lane == h0 + r, dr, 0.0)
            total = jnp.sum(jnp.where(own[0:1], dyx, 0.0), axis=1, keepdims=True)
            small[2:3, :] += jnp.where(lane1 == h0 + r, total, 0.0)
            dd = jnp.sum(jnp.where(own, dxx, 0.0), axis=1, keepdims=True)
            ddt[...] += jnp.where(lane == h0 + r, dd, 0.0)

        for k in range(1, ndp):
            to = lax.rem(dp + k, ndp)
            remote(
                partial.at[dp, j], partial.at[dp, j], ps_sem.at[to], pr_sem.at[dp], core, sec, to
            ).start()
        return 0

    lax.fori_loop(0, HALF, group, 0)

    def pass_on(slot, g, out, landed, s):
        part = relay.at[slot]
        remote(part, part, via_sem.at[0], relay_sem.at[slot], core, s, dp).wait_recv()
        remote(
            part, out.at[0, 0, :, pl.ds(g * WIDE, WIDE)], via_sem.at[0], landed, core, s, dp
        ).start()

    @pl.when(sec == 0)
    def _():
        for g in range(GROUPS):
            pass_on(g, g, ggate, gate_sem.at[1], 1)

    @pl.when(sec == 3)
    def _():
        for at in range(GROUPS // 2):
            pass_on(at, 2 * at + 1, nxt, next_sem.at[1], 2)

    damp = jnp.exp(dl_ref[...])
    dr16 = drate[:, 0:HEADS]
    dstep = (ddt[:, 0:HEADS] - dr16 * damp) * sigc[:, 0:HEADS]
    small[0:1, 0:HEADS] = jnp.sum(dstep, axis=0, keepdims=True)
    small[1:2, 0:HEADS] = jnp.sum(dr16 * ratec[:, 0:HEADS], axis=0, keepdims=True)
    drate[:, 0:HEADS] = dstep
    turned = drate[...].T
    for t in range(2):
        stage_s[t] = turned[0:HEADS, t * tok : (t + 1) * tok].astype(BF16)

    @pl.when(sec > 0)
    def _():
        for t in range(2):
            remote(
                stage_s.at[t], step_parts.at[core],
                dstep_sem.at[2], dstep_sem.at[core], t, sec - 1, dp,
            ).start()

    partial[dp, HALF, :, 0:128] = small[...]
    for k in range(1, ndp):
        to = lax.rem(dp + k, ndp)
        remote(
            partial.at[dp, HALF], partial.at[dp, HALF], ps_sem.at[to], pr_sem.at[dp], core, sec, to
        ).start()
    for k in range(1, ndp):
        to = lax.rem(dp + k, ndp)
        remote(partial.at[dp], partial.at[to], ps_sem.at[to], pr_sem.at[to], core, sec, to).wait()
    total = partial[0]
    for k in range(1, ndp):
        total = total + partial[k]
    final[core] = total
    halves = remote(final.at[core], final.at[core], fin_sem.at[0], fin_sem.at[1], other, sec, dp)
    halves.start()
    remote(final.at[core], final.at[other], fin_sem.at[0], fin_sem.at[1], other, sec, dp).wait()
    packed[...] = final[...]

    @pl.when(sec == 0)
    def _():
        pltpu.make_async_copy(zeros, nxt.at[0, 0], zero_sem.at[0]).wait()
        remote(relay, relay, via_sem.at[0], relay_sem.at[0], core, 1, dp).wait_send()

    @pl.when(sec > 0)
    def _():
        low = sec - 1
        remote(stage_c, stage_c, conv_sem.at[0], conv_sem.at[1], core, low, dp).wait_send()
        half_o = stage_o.at[:, :, pl.ds(0, WIDE)]
        remote(half_o, half_o, gate_sem.at[0], gate_sem.at[1], core, low, dp).wait_send()
        remote(stage_s, stage_s, dstep_sem.at[2], dstep_sem.at[0], core, low, dp).wait_send()
        remote(
            nxt.at[0, 0], nxt.at[0, 0], next_sem.at[0], next_sem.at[1], core, low, dp
        ).wait_recv()

    @pl.when(sec == nsec - 1)
    def _():
        whole = gconv.at[0, 0]
        pltpu.make_async_copy(whole, whole, zero_sem.at[1]).wait()
        pltpu.make_async_copy(zeros, ggate.at[0, 0], zero_sem.at[2]).wait()
        gstep[...] = jnp.zeros_like(gstep)
        used = relay.at[pl.ds(0, GROUPS // 2)]
        remote(used, used, via_sem.at[0], relay_sem.at[0], core, 2, dp).wait_send()

    @pl.when(sec < nsec - 1)
    def _():
        high = sec + 1
        half_o = stage_o.at[:, :, pl.ds(0, WIDE)]
        remote(half_o, half_o, next_sem.at[0], next_sem.at[1], core, high, dp).wait_send()
        for c in range(2):
            part = step_parts.at[c]
            remote(part, part, dstep_sem.at[2], dstep_sem.at[c], core, high, dp).wait_recv()
        gstep[0, 0] = (step_parts[0].astype(F32) + step_parts[1].astype(F32)).astype(BF16)
        whole = ggate.at[0, 0]
        remote(whole, whole, gate_sem.at[0], gate_sem.at[1], core, high, dp).wait_recv()
        whole = gconv.at[0, 0]
        remote(whole, whole, conv_sem.at[0], conv_sem.at[1], core, high, dp).wait_recv()


def finish_kernel(
    nxt_in, gconv_in, ggate_in, gstep_in, packed,
    nxt, gconv, ggate, gstep, gtap, gcb, gsb, gdl, gsk, gng,
    held, in_sem, out_sem,
):
    routes = [(nxt_in.at[0, 0], nxt.at[0, 0]), (ggate_in.at[0, 0], ggate.at[0, 0])]
    for part in range(5):
        cut = pl.ds(part * INNER, INNER)
        routes.append((gconv_in.at[0, 0, :, cut], gconv.at[0, 0, :, cut]))
    arrive = [pltpu.make_async_copy(r[0], held.at[i], in_sem.at[i]) for i, r in enumerate(routes)]
    leave = [pltpu.make_async_copy(held.at[i], r[1], out_sem.at[i]) for i, r in enumerate(routes)]
    for copy in arrive:
        copy.start()
    gstep[...] = gstep_in[...]
    for g in range(GROUPS):
        c, j = g // HALF, g % HALF
        gng[0:1, g * WIDE : (g + 1) * WIDE] = packed[c, j, 5:6, 0:WIDE]
        for off, width, col in (
            (0, WIDE, g * WIDE),
            (WIDE, STATE, INNER + g * STATE),
            (WIDE + STATE, STATE, INNER + (GROUPS + g) * STATE),
        ):
            gtap[0, :, col : col + width] = packed[c, j, 0:CONV, off : off + width]
            gcb[0:1, col : col + width] = packed[c, j, CONV : CONV + 1, off : off + width]
    for at, ref in enumerate((gsb, gdl, gsk)):
        ref[...] = packed[0, HALF, at : at + 1, 0:HEADS] + packed[1, HALF, at : at + 1, 0:HEADS]
    for into, out in zip(arrive, leave):
        into.wait()
        out.start()
    for out in leave:
        out.wait()


def paired(
    conv_input, gate_input, step_input, cotangent, conv_weight,
    conv_bias, step_bias, decay_log, skip_gain, norm_gain,
):
    tok = conv_input.shape[2]
    seq = 2 * tok
    ndp = lax.axis_size("dp")
    hbm = pl.BlockSpec(memory_space=pl.ANY)
    vmem = pl.BlockSpec(memory_space=pltpu.VMEM)
    like = lambda a, kind: jax.ShapeDtypeStruct(a.shape, kind)
    scratch = [
        pltpu.VMEM((HALF, seq, MIX + 2 * WIDE), BF16),
        pltpu.VMEM((2, HEADS, tok), BF16),
        pltpu.VMEM((128, seq), F32),
        pltpu.VMEM((seq + 8, MIX), F32),
        pltpu.VMEM((seq + 8, MIX), F32),
        pltpu.VMEM((seq, MIX), F32),
        pltpu.VMEM((seq, MIX), F32),
        pltpu.VMEM((seq, 128), F32),
        pltpu.VMEM((seq, 128), F32),
        pltpu.VMEM((seq, 128), F32),
        pltpu.VMEM((seq, 128), F32),
        pltpu.VMEM((128, seq), F32),
        pltpu.VMEM((seq, 128), F32),
        pltpu.VMEM((seq, 128), F32),
        pltpu.VMEM((8, 128), F32),
        pltpu.VMEM((HALF, seq, MIX), BF16),
        pltpu.VMEM((HALF, seq, 2 * WIDE), BF16),
        pltpu.VMEM((2, HEADS, tok), BF16),
        pltpu.VMEM((2, HEADS, tok), BF16),
        pltpu.VMEM((ndp, HALF + 1, 8, MIX), F32),
        pltpu.VMEM((2, HALF + 1, 8, MIX), F32),
        pltpu.VMEM((tok, INNER), BF16),
        pltpu.VMEM((GROUPS, tok, WIDE), BF16),
        pltpu.SemaphoreType.DMA((HALF,)),
        pltpu.SemaphoreType.DMA((HALF,)),
        pltpu.SemaphoreType.DMA((HALF,)),
        pltpu.SemaphoreType.DMA((3,)),
        pltpu.SemaphoreType.DMA((2,)),
        pltpu.SemaphoreType.DMA((2,)),
        pltpu.SemaphoreType.DMA((2,)),
        pltpu.SemaphoreType.DMA((3,)),
        pltpu.SemaphoreType.DMA((ndp,)),
        pltpu.SemaphoreType.DMA((ndp,)),
        pltpu.SemaphoreType.DMA((2,)),
        pltpu.SemaphoreType.DMA((3,)),
        pltpu.SemaphoreType.DMA((1,)),
        pltpu.SemaphoreType.DMA((GROUPS,)),
    ]
    turned = jnp.swapaxes(step_input, 2, 3)
    sent = pl.pallas_call(
        pair_kernel,
        name="mixer_tick",
        in_specs=[hbm] * 4 + [vmem] * 6,
        out_specs=[hbm] * 3 + [vmem] * 2,
        out_shape=[
            like(gate_input, BF16),
            like(conv_input, BF16),
            like(gate_input, BF16),
            like(turned, BF16),
            jax.ShapeDtypeStruct((2, HALF + 1, 8, MIX), F32),
        ],
        scratch_shapes=scratch,
        compiler_params=pltpu.CompilerParams(collective_id=0, has_side_effects=True),
    )(
        conv_input, gate_input, turned, cotangent, conv_weight,
        conv_bias, step_bias, decay_log, skip_gain, norm_gain,
    )
    done = pl.pallas_call(
        finish_kernel,
        name="mixer_finish",
        in_specs=[hbm] * 3 + [vmem] * 2,
        out_specs=[hbm] * 3 + [vmem] * 7,
        out_shape=[
            like(gate_input, BF16),
            like(conv_input, BF16),
            like(gate_input, BF16),
            like(turned, BF16),
            like(conv_weight, F32),
            like(conv_bias, F32),
            like(step_bias, F32),
            like(decay_log, F32),
            like(skip_gain, F32),
            like(norm_gain, F32),
        ],
        scratch_shapes=[
            pltpu.VMEM((7, tok, INNER), BF16),
            pltpu.SemaphoreType.DMA((7,)),
            pltpu.SemaphoreType.DMA((7,)),
        ],
    )(*sent)
    return tuple(done[:3]) + (jnp.swapaxes(done[3], 2, 3),) + tuple(done[4:])


def solution(mesh):
    in_specs = (
        P("section", "dp", "ctx", None),
        P("section", "dp", "ctx", None),
        P("section", "dp", "ctx", None),
        P("section", "dp", "ctx", None),
        P("section", None, None),
        P("section", None),
        P("section", None),
        P("section", None),
        P("section", None),
        P("section", None),
    )
    out_specs = (
        P("section", "dp", "ctx", None),
        P("section", "dp", "ctx", None),
        P("section", "dp", "ctx", None),
        P("section", "dp", "ctx", None),
        P("section", None, None),
        P("section", None),
        P("section", None),
        P("section", None),
        P("section", None),
        P("section", None),
    )
    body = paired if (mesh.shape["ctx"], mesh.shape["section"]) == (2, 4) else shards
    return jax.shard_map(body, mesh=mesh, in_specs=in_specs, out_specs=out_specs, check_vma=False)
```

```python
import functools
import jax
import jax.numpy as jnp
from jax import lax
from jax.experimental import pallas as pl
from jax.experimental.pallas import tpu as pltpu
from jax.sharding import PartitionSpec as P

HEADS = 16
HEAD_DIM = 64
STATE = 256
GROUPS = 8
CONV = 4


HIGH_BOUND = lax.Precision.HIGHEST


def shifted(block, axis, distance):
    devices = range(lax.axis_size(axis))
    route = [(i - distance, i) for i in devices if i - distance in devices]
    return lax.ppermute(block, axis, route)


def prefix(part, axis, combine, identity):
    count = lax.axis_size(axis)
    place = lax.axis_index(axis)
    ahead = count - 1 - place
    gathered = jax.tree.map(lambda a: lax.all_gather(a, axis), part)
    state = jax.tree.map(lambda a, e: jnp.zeros_like(a) + jnp.asarray(e, a.dtype), part, identity)

    def one(turn, state):
        source = count - 1 - turn
        return combine(
            state, jax.tree.map(lambda a: lax.dynamic_index_in_dim(a, source, 0, False), gathered)
        )

    return lax.fori_loop(0, ahead, one, state)


def conv_mix(extended, taps, initial_offset):
    rows = extended.shape[0] - (CONV - 1)
    total = initial_offset[None, :]
    for tap in range(CONV):
        total = total + taps[tap][None, :] * extended[tap : tap + rows]
    return jax.nn.silu(total)


def split_mix(mixed, steps, step_shift, damping_exponents):
    rows = mixed.shape[0]
    inner = HEADS * HEAD_DIM
    payload_lines = mixed[:, :inner].reshape(rows, GROUPS, HEADS // GROUPS, HEAD_DIM)
    in_maps = mixed[:, inner : inner + GROUPS * STATE].reshape(rows, GROUPS, STATE)
    out_maps = mixed[:, inner + GROUPS * STATE :].reshape(rows, GROUPS, STATE)
    delta = jax.nn.softplus(steps + step_shift[None, :])
    cumulative = jnp.cumsum(delta * (-jnp.exp(damping_exponents))[None, :], axis=0)
    return (payload_lines, in_maps, out_maps, delta, cumulative)


def fragment_condition(extended, steps, taps, initial_offset, step_shift, damping_exponents):
    payload_lines, in_maps, out_maps, delta, cumulative = split_mix(
        conv_mix(extended, taps, initial_offset), steps, step_shift, damping_exponents
    )
    rows = payload_lines.shape[0]
    total = cumulative[-1]
    weight = (jnp.exp(total[None, :] - cumulative) * delta).reshape(rows, GROUPS, HEADS // GROUPS)
    state = jnp.einsum(
        "tgrp,tgn->grpn", payload_lines * weight[..., None], in_maps, precision=HIGH_BOUND
    )
    return (state.reshape(HEADS, HEAD_DIM, STATE), total)


def shard_layer(
    extended,
    gates,
    steps,
    taps,
    initial_offset,
    step_shift,
    damping_exponents,
    skip_values,
    gain_values,
    carried,
):
    payload_lines, in_maps, out_maps, delta, cumulative = split_mix(
        conv_mix(extended, taps, initial_offset), steps, step_shift, damping_exponents
    )
    rows = payload_lines.shape[0]
    reps = HEADS // GROUPS
    lower = (jnp.arange(rows)[:, None] >= jnp.arange(rows)[None, :])[None]
    seg = cumulative.T[:, :, None] - cumulative.T[:, None, :]
    weight = jnp.exp(jnp.where(lower, seg, -jnp.inf)).reshape(GROUPS, reps, rows, rows)
    intersection_maps = jnp.einsum("tgn,sgn->gts", out_maps, in_maps, precision=HIGH_BOUND)
    score_matrix = weight * intersection_maps[:, None]
    scaled_values = payload_lines * delta.reshape(rows, GROUPS, reps)[..., None]
    final_output = jnp.einsum("jzlh,hjzc->ljzc", score_matrix, scaled_values, precision=HIGH_BOUND)
    incoming = jnp.einsum(
        "tgn,grpn->tgrp",
        out_maps,
        carried.reshape(GROUPS, reps, HEAD_DIM, STATE),
        precision=HIGH_BOUND,
    )
    final_output = (
        final_output + incoming * jnp.exp(cumulative).reshape(rows, GROUPS, reps)[..., None]
    )
    final_output = (
        final_output + skip_values.reshape(GROUPS, reps)[None, :, :, None] * payload_lines
    )
    gated = final_output.reshape(rows, GROUPS, -1) * jax.nn.silu(gates).reshape(rows, GROUPS, -1)
    normed = gated * lax.rsqrt(jnp.mean(gated * gated, axis=-1, keepdims=True) + 1e-05)
    return normed.reshape(rows, -1) * gain_values[None, :]


def combine(earlier, later):
    return (earlier[0] * later[0], later[0][:, None] * earlier[1] + later[1])


def shards(
    conv_input,
    gate_input,
    step_input,
    cotangent,
    conv_weight,
    conv_bias,
    step_bias,
    decay_log,
    skip_gain,
    norm_gain,
):
    local_rows = conv_input[0, 0]
    count = local_rows.shape[0]
    taps, initial_offset = (conv_weight[0], conv_bias[0])
    step_shift, damping_exponents = (step_bias[0], decay_log[0])
    skip_values, gain_values = (skip_gain[0], norm_gain[0])
    previous = shifted(local_rows[count - (CONV - 1) :], "ctx", 1)
    extended = jnp.concatenate([previous, local_rows], 0).astype(jnp.float32)
    gates = gate_input[0, 0].astype(jnp.float32)
    steps = step_input[0, 0].astype(jnp.float32)
    (state, total), state_pull = jax.vjp(
        fragment_condition, extended, steps, taps, initial_offset, step_shift, damping_exponents
    )
    decay = jnp.exp(total)
    flat_state = state.reshape(HEADS, HEAD_DIM * STATE)
    unity = (jnp.ones((HEADS,), jnp.float32), jnp.zeros((HEADS, HEAD_DIM * STATE), jnp.float32))

    def advance(index, current):
        return shifted(decay[:, None] * current + flat_state, "ctx", 1)

    incoming = lax.fori_loop(
        0, lax.axis_size("ctx") - 1, advance, jnp.zeros((HEADS, HEAD_DIM * STATE), jnp.float32)
    )
    carried = incoming.reshape(HEADS, HEAD_DIM, STATE)
    final_output, layer_pull = jax.vjp(
        shard_layer,
        extended,
        gates,
        steps,
        taps,
        initial_offset,
        step_shift,
        damping_exponents,
        skip_values,
        gain_values,
        carried,
    )
    forward = shifted(final_output.astype(jnp.bfloat16)[None, None], "section", 1)
    grads = layer_pull(cotangent[0, 0].astype(jnp.float32))
    carry_grad = grads[9].reshape(HEADS, HEAD_DIM * STATE)
    outgoing = prefix((decay, carry_grad), "ctx", combine, unity)[1]
    outgoing_grad = outgoing.reshape(HEADS, HEAD_DIM, STATE)
    total_grad = jnp.sum(outgoing_grad * carried, axis=(1, 2)) * decay
    extra = state_pull((outgoing_grad, total_grad))
    ext_grad = grads[0] + extra[0]
    step_grad = grads[2] + extra[1]
    param_terms = (
        grads[3] + extra[2],
        grads[4] + extra[3],
        grads[5] + extra[4],
        grads[6] + extra[5],
        grads[7],
        grads[8],
    )
    returned = shifted(ext_grad[: CONV - 1], "ctx", -1)
    own_grad = ext_grad[CONV - 1 :]
    row_grad = jnp.concatenate(
        [own_grad[: count - (CONV - 1)], own_grad[count - (CONV - 1) :] + returned], 0
    )
    backward = shifted(
        (
            row_grad.astype(jnp.bfloat16)[None, None],
            grads[1].astype(jnp.bfloat16)[None, None],
            step_grad.astype(jnp.bfloat16)[None, None],
        ),
        "section",
        -1,
    )
    summed = lax.psum(
        (
            param_terms[0],
            param_terms[1],
            param_terms[2],
            param_terms[3],
            param_terms[4],
            param_terms[5],
        ),
        ("ctx", "dp"),
    )
    return (
        forward,
        backward[0],
        backward[1],
        backward[2],
        summed[0][None],
        summed[1][None],
        summed[2][None],
        summed[3][None],
        summed[4][None],
        summed[5][None],
    )


MESH = pl.DeviceIdType.MESH
F32 = jnp.float32
BF16 = jnp.bfloat16
INNER = HEADS * HEAD_DIM
REPS = HEADS // GROUPS
WIDE = REPS * HEAD_DIM
MIX = WIDE + 2 * STATE
HALF = GROUPS // 2
NN = ((1,), (0,))
NT = ((1,), (1,))
TN = ((0,), (0,))


def split(a):
    high = a.astype(BF16)
    return high, (a - high.astype(F32)).astype(BF16)


def dot(a, b, dims):
    return lax.dot_general(a, b, (dims, ((), ())), preferred_element_type=F32)


def dot3(a, b, dims):
    return dot(a[0], b[0], dims) + (dot(a[0], b[1], dims) + dot(a[1], b[0], dims))


def group_columns(g):
    return (
        pl.multiple_of(g * WIDE, 128),
        pl.multiple_of(INNER + g * STATE, 128),
        pl.multiple_of(INNER + (GROUPS + g) * STATE, 128),
    )


def pair_kernel(
    conv_in, gate_in, step_in, cot_in, w_ref, b_ref, sb_ref, dl_ref, sk_ref, ng_ref,
    nxt, gconv, ggate, gstep, packed,
    uin, steps, steprow, upad, zpad, mix, dsl, dtc, sigc, ratec, cumc, cumr, ddt, drate, small,
    stage_c, stage_o, stage_s, step_parts, partial, final, zeros, relay, step_out,
    own_sem, xs_sem, xr_sem, st_sem, conv_sem, gate_sem, next_sem, dstep_sem,
    ps_sem, pr_sem, fin_sem, zero_sem, via_sem, relay_sem,
):
    core = lax.axis_index("ctx")
    sec = lax.axis_index("section")
    dp = lax.axis_index("dp")
    nsec = lax.axis_size("section")
    ndp = lax.axis_size("dp")
    tok = conv_in.shape[2]
    seq = 2 * tok
    other = 1 - core

    def place(c, s, d):
        return {"ctx": c, "section": s, "dp": d}

    def remote(src, dst, send, recv, c, s, d):
        return pltpu.make_async_remote_copy(
            src_ref=src, dst_ref=dst, send_sem=send, recv_sem=recv,
            device_id=place(c, s, d), device_id_type=MESH,
        )

    after = lax.rem(sec + 1, nsec)
    before = lax.rem(sec + nsec - 1, nsec)
    barrier = pltpu.get_barrier_semaphore()

    def greet(c, s, d):
        pl.semaphore_signal(barrier, inc=1, device_id=place(c, s, d), device_id_type=MESH)

    greet(other, sec, dp)
    for c in range(2):
        greet(c, after, dp)
        greet(c, before, dp)
        greet(c, lax.rem(sec + 2, nsec), dp)
    for k in range(1, ndp):
        greet(core, sec, lax.rem(dp + k, ndp))

    def pieces(g):
        xc, bc, cc = group_columns(g)
        return (
            (conv_in.at[0, 0, :, pl.ds(xc, WIDE)], 0, WIDE),
            (conv_in.at[0, 0, :, pl.ds(bc, STATE)], WIDE, STATE),
            (conv_in.at[0, 0, :, pl.ds(cc, STATE)], WIDE + STATE, STATE),
            (gate_in.at[0, 0, :, pl.ds(xc, WIDE)], MIX, WIDE),
            (cot_in.at[0, 0, :, pl.ds(xc, WIDE)], MIX + WIDE, WIDE),
        )

    mine = pl.ds(pl.multiple_of(core * tok, tok), tok)
    theirs = pl.ds(pl.multiple_of(other * tok, tok), tok)
    own_step = pltpu.make_async_copy(step_in.at[0, 0], steps.at[core], st_sem.at[0])
    own_step.start()

    def fetch(j, _):
        for src, off, width in pieces(core * HALF + j):
            pltpu.make_async_copy(
                src, uin.at[j, mine, pl.ds(off, width)], own_sem.at[j]
            ).start()
        return 0

    lax.fori_loop(0, HALF, fetch, 0)
    zeros[...] = jnp.zeros_like(zeros)
    partial[dp] = jnp.zeros(partial.shape[1:], F32)
    upad[0:8, :] = jnp.zeros((8, MIX), F32)
    zpad[seq : seq + 8, :] = jnp.zeros((8, MIX), F32)
    for ref in (steprow, dtc, sigc, ratec, ddt, drate, small):
        ref[...] = jnp.zeros_like(ref)
    pl.semaphore_wait(barrier, 1 + 6 + (ndp - 1))
    step_copy = remote(
        step_in.at[0, 0], steps.at[core], st_sem.at[1], st_sem.at[2], other, sec, dp
    )
    step_copy.start()

    def exchange(j, _):
        for src, off, width in pieces(other * HALF + j):
            remote(
                src, uin.at[j, mine, pl.ds(off, width)], xs_sem.at[j], xr_sem.at[j], other, sec, dp
            ).start()
        return 0

    lax.fori_loop(0, HALF, exchange, 0)

    @pl.when(sec == 0)
    def _():
        pltpu.make_async_copy(zeros, nxt.at[0, 0], zero_sem.at[0]).start()

    @pl.when(sec == nsec - 1)
    def _():
        for part in range(5):
            pltpu.make_async_copy(
                zeros, gconv.at[0, 0, :, pl.ds(part * INNER, INNER)], zero_sem.at[1]
            ).start()
        pltpu.make_async_copy(zeros, ggate.at[0, 0], zero_sem.at[2]).start()

    own_step.wait()
    step_copy.wait()
    for c in range(2):
        steprow[0:HEADS, c * tok : (c + 1) * tok] = steps[c].astype(F32)
    raw = steprow[...].T[:, 0:HEADS] + sb_ref[...]
    delta = jnp.maximum(raw, 0.0) + jnp.log1p(jnp.exp(-jnp.abs(raw)))
    dtc[:, 0:HEADS] = delta
    sigc[:, 0:HEADS] = jax.nn.sigmoid(raw)
    ratec[:, 0:HEADS] = delta * (-jnp.exp(dl_ref[...]))
    rows2 = lax.broadcasted_iota(jnp.int32, (seq, seq), 0)
    cols2 = lax.broadcasted_iota(jnp.int32, (seq, seq), 1)
    ones_low = jnp.where(rows2 >= cols2, 1.0, 0.0).astype(BF16)
    rate = ratec[...]
    r_hi, r_rest = rate.astype(BF16), rate - rate.astype(BF16).astype(F32)
    r_mid, r_lo = split(r_rest)
    cumulative = dot(ones_low, r_hi, NN) + (dot(ones_low, r_mid, NN) + dot(ones_low, r_lo, NN))
    cumc[...] = cumulative
    cumr[...] = cumulative.T

    def group(j, _):
        g = core * HALF + j
        cols = group_columns(g)
        pltpu.make_async_copy(uin.at[j, mine], uin.at[j, mine], own_sem.at[j]).wait()
        remote(uin.at[j, mine], uin.at[j, theirs], xs_sem.at[j], xr_sem.at[j], other, sec, dp).wait()
        blocks = [(0, cols[0])]
        for base, col in ((WIDE, cols[1]), (WIDE + STATE, cols[2])):
            for part in range(STATE // 128):
                blocks.append((base + part * 128, pl.multiple_of(col + part * 128, 128)))

        for off, col in blocks:
            here = slice(off, off + 128)
            upad[8 : 8 + seq, here] = uin[j, :, here].astype(F32)
            z = b_ref[:, pl.ds(col, 128)]
            for k in range(CONV):
                z = z + w_ref[0, pl.ds(k, 1), pl.ds(col, 128)] * upad[5 + k : 5 + k + seq, here]
            s = jax.nn.sigmoid(z)
            mix[:, here] = z * s
            dsl[:, here] = s * (1.0 + z * (1.0 - s))

        lane = lax.broadcasted_iota(jnp.int32, (seq, 128), 1)
        lane1 = lax.broadcasted_iota(jnp.int32, (1, 128), 1)
        lane16 = lax.broadcasted_iota(jnp.int32, (1, HEADS), 1)
        row = lax.broadcasted_iota(jnp.int32, (seq, seq), 0)
        column = lax.broadcasted_iota(jnp.int32, (seq, seq), 1)
        first = lane < HEAD_DIM

        def pick(ref, h):
            return jnp.sum(jnp.where(lane == h, ref[...], 0.0), axis=1, keepdims=True)

        def pick1(ref, h):
            return jnp.sum(jnp.where(lane16 == h, ref[...], 0.0), axis=1, keepdims=True)

        x = mix[:, 0:WIDE]
        bmap = split(mix[:, WIDE : WIDE + STATE])
        cmap = split(mix[:, WIDE + STATE : MIX])
        h0 = g * REPS
        dt2 = jnp.where(first, pick(dtc, h0), pick(dtc, h0 + 1))
        skip2 = jnp.where(first[0:1], pick1(sk_ref, h0), pick1(sk_ref, h0 + 1))
        xs = x * dt2
        xs_p = split(xs)
        scores = dot3(cmap, bmap, NT)
        decay, mixed, ys = [], [], []
        for r in range(REPS):
            seg = pick(cumc, h0 + r) - cumr[pl.ds(h0 + r, 1), :]
            w = jnp.exp(jnp.where(row >= column, seg, -jnp.inf))
            a = scores * w
            a_p = split(a)
            decay.append(w)
            mixed.append((a, a_p))
            ys.append(dot3(a_p, xs_p, NN))
        y = jnp.where(first, ys[0], ys[1]) + skip2 * x
        gate = uin[j, :, MIX : MIX + WIDE].astype(F32)
        cot = uin[j, :, MIX + WIDE : MIX + 2 * WIDE].astype(F32)
        gain = ng_ref[:, pl.ds(cols[0], WIDE)]
        s = jax.nn.sigmoid(gate)
        act = gate * s
        gated = y * act
        scale = lax.rsqrt(jnp.mean(gated * gated, axis=1, keepdims=True) + 1e-05)
        normed = gated * scale
        stage_o[j, :, 0:WIDE] = (normed * gain).astype(BF16)
        dn = cot * gain
        dgated = scale * (dn - normed * jnp.mean(dn * normed, axis=1, keepdims=True))
        dy = dgated * act
        stage_o[j, :, WIDE : 2 * WIDE] = (dgated * y * (s * (1.0 + gate * (1.0 - s)))).astype(BF16)

        odd = lax.rem(j, 2) == 1

        def send_half(base, t, dst, done, landed, s):
            remote(
                stage_o.at[j, pl.ds(t * tok, tok), pl.ds(base, WIDE)], dst, done, landed, t, s, dp
            ).start()

        @pl.when(jnp.logical_and(sec < nsec - 1, jnp.logical_not(jnp.logical_and(sec == 1, odd))))
        def _():
            for t in range(2):
                send_half(
                    0, t, nxt.at[0, 0, :, pl.ds(cols[0], WIDE)],
                    next_sem.at[0], next_sem.at[1], sec + 1,
                )

        @pl.when(jnp.logical_and(sec == 1, odd))
        def _():
            slot = core * (HALF // 2) + j // 2
            for t in range(2):
                send_half(0, t, relay.at[slot], next_sem.at[0], relay_sem.at[slot], 3)

        @pl.when(jnp.logical_or(sec == 1, sec == 3))
        def _():
            for t in range(2):
                send_half(
                    WIDE, t, ggate.at[0, 0, :, pl.ds(cols[0], WIDE)],
                    gate_sem.at[0], gate_sem.at[1], sec - 1,
                )

        @pl.when(sec == 2)
        def _():
            slot = core * HALF + j
            for t in range(2):
                send_half(WIDE, t, relay.at[slot], gate_sem.at[0], relay_sem.at[slot], 0)

        partial[dp, j, 5:6, 0:WIDE] = jnp.sum(cot * normed, axis=0, keepdims=True)
        dyx = jnp.sum(dy * x, axis=0, keepdims=True)
        dscore = jnp.zeros((seq, seq), F32)
        dy_p = split(dy)
        das = []
        for r in range(REPS):
            own = first if r == 0 else jnp.logical_not(first)
            da = dot3(split(jnp.where(own, dy, 0.0)), xs_p, NT)
            das.append(da)
            dscore = dscore + da * decay[r]
        ds_p = split(dscore)

        def conv_back(off, width, start):
            for part in range(width // 128):
                here = slice(off + part * 128, off + part * 128 + 128)
                col = pl.multiple_of(start + part * 128, 128)
                dz = zpad[0:seq, here]
                du = jnp.zeros((seq, 128), F32)
                for k in range(CONV):
                    du = du + w_ref[0, pl.ds(k, 1), pl.ds(col, 128)] * zpad[3 - k : 3 - k + seq, here]
                    partial[dp, j, pl.ds(k, 1), here] = jnp.sum(
                        dz * upad[5 + k : 5 + k + seq, here], axis=0, keepdims=True
                    )
                partial[dp, j, pl.ds(4, 1), here] = jnp.sum(dz, axis=0, keepdims=True)
                stage_c[j, :, here] = du.astype(BF16)

            @pl.when(sec > 0)
            def _():
                for t in range(2):
                    remote(
                        stage_c.at[j, pl.ds(t * tok, tok), pl.ds(off, width)],
                        gconv.at[0, 0, :, pl.ds(start, width)],
                        conv_sem.at[0], conv_sem.at[1], t, sec - 1, dp,
                    ).start()

        zpad[0:seq, WIDE + STATE : MIX] = dot3(ds_p, bmap, NN) * dsl[:, WIDE + STATE : MIX]
        conv_back(WIDE + STATE, STATE, cols[2])
        zpad[0:seq, WIDE : WIDE + STATE] = dot3(ds_p, cmap, TN) * dsl[:, WIDE : WIDE + STATE]
        conv_back(WIDE, STATE, cols[1])
        dxs = jnp.where(first, dot3(mixed[0][1], dy_p, TN), dot3(mixed[1][1], dy_p, TN))
        zpad[0:seq, 0:WIDE] = (skip2 * dy + dxs * dt2) * dsl[:, 0:WIDE]
        conv_back(0, WIDE, cols[0])
        upper = jnp.where(row <= column, 1.0, 0.0).astype(BF16)
        dxx = dxs * x
        for r in range(REPS):
            own = first if r == 0 else jnp.logical_not(first)
            p = split(das[r] * mixed[r][0])
            later = dot(upper, p[0], NN) + dot(upper, p[1], NN)
            dr = jnp.sum(jnp.where(row > column, later, 0.0), axis=1, keepdims=True)
            drate[...] += jnp.where(lane == h0 + r, dr, 0.0)
            total = jnp.sum(jnp.where(own[0:1], dyx, 0.0), axis=1, keepdims=True)
            small[2:3, :] += jnp.where(lane1 == h0 + r, total, 0.0)
            dd = jnp.sum(jnp.where(own, dxx, 0.0), axis=1, keepdims=True)
            ddt[...] += jnp.where(lane == h0 + r, dd, 0.0)

        for k in range(1, ndp):
            to = lax.rem(dp + k, ndp)
            remote(
                partial.at[dp, j], partial.at[dp, j], ps_sem.at[to], pr_sem.at[dp], core, sec, to
            ).start()
        return 0

    lax.fori_loop(0, HALF, group, 0)

    def pass_on(slot, g, out, landed, s):
        part = relay.at[slot]
        remote(part, part, via_sem.at[0], relay_sem.at[slot], core, s, dp).wait_recv()
        remote(
            part, out.at[0, 0, :, pl.ds(g * WIDE, WIDE)], via_sem.at[0], landed, core, s, dp
        ).start()

    @pl.when(sec == 0)
    def _():
        for g in range(GROUPS):
            pass_on(g, g, ggate, gate_sem.at[1], 1)

    @pl.when(sec == 3)
    def _():
        for at in range(GROUPS // 2):
            pass_on(at, 2 * at + 1, nxt, next_sem.at[1], 2)

    damp = jnp.exp(dl_ref[...])
    dr16 = drate[:, 0:HEADS]
    dstep = (ddt[:, 0:HEADS] - dr16 * damp) * sigc[:, 0:HEADS]
    small[0:1, 0:HEADS] = jnp.sum(dstep, axis=0, keepdims=True)
    small[1:2, 0:HEADS] = jnp.sum(dr16 * ratec[:, 0:HEADS], axis=0, keepdims=True)
    drate[:, 0:HEADS] = dstep
    turned = drate[...].T
    for t in range(2):
        stage_s[t] = turned[0:HEADS, t * tok : (t + 1) * tok].astype(BF16)

    @pl.when(sec > 0)
    def _():
        for t in range(2):
            remote(
                stage_s.at[t], step_parts.at[core],
                dstep_sem.at[2], dstep_sem.at[core], t, sec - 1, dp,
            ).start()

    partial[dp, HALF, :, 0:128] = small[...]
    for k in range(1, ndp):
        to = lax.rem(dp + k, ndp)
        remote(
            partial.at[dp, HALF], partial.at[dp, HALF], ps_sem.at[to], pr_sem.at[dp], core, sec, to
        ).start()
    for k in range(1, ndp):
        to = lax.rem(dp + k, ndp)
        remote(partial.at[dp], partial.at[to], ps_sem.at[to], pr_sem.at[to], core, sec, to).wait()
    total = partial[0]
    for k in range(1, ndp):
        total = total + partial[k]
    final[core] = total
    halves = remote(final.at[core], final.at[core], fin_sem.at[0], fin_sem.at[1], other, sec, dp)
    halves.start()
    remote(final.at[core], final.at[other], fin_sem.at[0], fin_sem.at[1], other, sec, dp).wait()
    to_packed = pltpu.make_async_copy(final, packed, own_sem.at[0])
    to_packed.start()

    @pl.when(sec == nsec - 1)
    def _():
        step_out[...] = jnp.zeros_like(step_out)

    @pl.when(sec < nsec - 1)
    def _():
        for c in range(2):
            part = step_parts.at[c]
            remote(part, part, dstep_sem.at[2], dstep_sem.at[c], core, sec + 1, dp).wait_recv()
        step_out[...] = (step_parts[0].astype(F32) + step_parts[1].astype(F32)).astype(BF16)

    to_step = pltpu.make_async_copy(step_out, gstep.at[0, 0], own_sem.at[1])
    to_step.start()

    @pl.when(sec == 0)
    def _():
        pltpu.make_async_copy(zeros, nxt.at[0, 0], zero_sem.at[0]).wait()
        remote(relay, relay, via_sem.at[0], relay_sem.at[0], core, 1, dp).wait_send()

    @pl.when(sec > 0)
    def _():
        low = sec - 1
        remote(stage_c, stage_c, conv_sem.at[0], conv_sem.at[1], core, low, dp).wait_send()
        half_o = stage_o.at[:, :, pl.ds(0, WIDE)]
        remote(half_o, half_o, gate_sem.at[0], gate_sem.at[1], core, low, dp).wait_send()
        remote(stage_s, stage_s, dstep_sem.at[2], dstep_sem.at[0], core, low, dp).wait_send()
        remote(
            nxt.at[0, 0], nxt.at[0, 0], next_sem.at[0], next_sem.at[1], core, low, dp
        ).wait_recv()

    @pl.when(sec == nsec - 1)
    def _():
        whole = gconv.at[0, 0]
        pltpu.make_async_copy(whole, whole, zero_sem.at[1]).wait()
        pltpu.make_async_copy(zeros, ggate.at[0, 0], zero_sem.at[2]).wait()
        used = relay.at[pl.ds(0, GROUPS // 2)]
        remote(used, used, via_sem.at[0], relay_sem.at[0], core, 2, dp).wait_send()

    @pl.when(sec < nsec - 1)
    def _():
        high = sec + 1
        half_o = stage_o.at[:, :, pl.ds(0, WIDE)]
        remote(half_o, half_o, next_sem.at[0], next_sem.at[1], core, high, dp).wait_send()
        whole = ggate.at[0, 0]
        remote(whole, whole, gate_sem.at[0], gate_sem.at[1], core, high, dp).wait_recv()
        whole = gconv.at[0, 0]
        remote(whole, whole, conv_sem.at[0], conv_sem.at[1], core, high, dp).wait_recv()

    to_packed.wait()
    to_step.wait()


def finish_kernel(
    nxt_in, gconv_in, ggate_in, gstep_in, packed_in,
    nxt, gconv, ggate, gstep, gtap, gcb, gsb, gdl, gsk, gng,
    held, held_step, packed, in_sem, out_sem,
):
    routes = [
        (gstep_in.at[0, 0], held_step, gstep.at[0, 0]),
        (nxt_in.at[0, 0], held.at[0], nxt.at[0, 0]),
        (ggate_in.at[0, 0], held.at[1], ggate.at[0, 0]),
    ]
    for part in range(5):
        cut = pl.ds(part * INNER, INNER)
        routes.append((gconv_in.at[0, 0, :, cut], held.at[2 + part], gconv.at[0, 0, :, cut]))
    arrive = [pltpu.make_async_copy(a, b, in_sem.at[i]) for i, (a, b, _) in enumerate(routes)]
    leave = [pltpu.make_async_copy(b, c, out_sem.at[i]) for i, (_, b, c) in enumerate(routes)]
    first = pltpu.make_async_copy(packed_in, packed, in_sem.at[8])
    first.start()
    for copy in arrive:
        copy.start()
    for into, out in zip(arrive, leave):
        into.wait()
        out.start()
    first.wait()
    for g in range(GROUPS):
        c, j = g // HALF, g % HALF
        gng[0:1, g * WIDE : (g + 1) * WIDE] = packed[c, j, 5:6, 0:WIDE]
        for off, width, col in (
            (0, WIDE, g * WIDE),
            (WIDE, STATE, INNER + g * STATE),
            (WIDE + STATE, STATE, INNER + (GROUPS + g) * STATE),
        ):
            gtap[0, :, col : col + width] = packed[c, j, 0:CONV, off : off + width]
            gcb[0:1, col : col + width] = packed[c, j, CONV : CONV + 1, off : off + width]
    for at, ref in enumerate((gsb, gdl, gsk)):
        ref[...] = packed[0, HALF, at : at + 1, 0:HEADS] + packed[1, HALF, at : at + 1, 0:HEADS]
    for out in leave:
        out.wait()


def paired(
    conv_input, gate_input, step_input, cotangent, conv_weight,
    conv_bias, step_bias, decay_log, skip_gain, norm_gain,
):
    tok = conv_input.shape[2]
    seq = 2 * tok
    ndp = lax.axis_size("dp")
    hbm = pl.BlockSpec(memory_space=pl.ANY)
    vmem = pl.BlockSpec(memory_space=pltpu.VMEM)
    like = lambda a, kind: jax.ShapeDtypeStruct(a.shape, kind)
    scratch = [
        pltpu.VMEM((HALF, seq, MIX + 2 * WIDE), BF16),
        pltpu.VMEM((2, HEADS, tok), BF16),
        pltpu.VMEM((128, seq), F32),
        pltpu.VMEM((seq + 8, MIX), F32),
        pltpu.VMEM((seq + 8, MIX), F32),
        pltpu.VMEM((seq, MIX), F32),
        pltpu.VMEM((seq, MIX), F32),
        pltpu.VMEM((seq, 128), F32),
        pltpu.VMEM((seq, 128), F32),
        pltpu.VMEM((seq, 128), F32),
        pltpu.VMEM((seq, 128), F32),
        pltpu.VMEM((128, seq), F32),
        pltpu.VMEM((seq, 128), F32),
        pltpu.VMEM((seq, 128), F32),
        pltpu.VMEM((8, 128), F32),
        pltpu.VMEM((HALF, seq, MIX), BF16),
        pltpu.VMEM((HALF, seq, 2 * WIDE), BF16),
        pltpu.VMEM((2, HEADS, tok), BF16),
        pltpu.VMEM((2, HEADS, tok), BF16),
        pltpu.VMEM((ndp, HALF + 1, 8, MIX), F32),
        pltpu.VMEM((2, HALF + 1, 8, MIX), F32),
        pltpu.VMEM((tok, INNER), BF16),
        pltpu.VMEM((GROUPS, tok, WIDE), BF16),
        pltpu.VMEM((HEADS, tok), BF16),
        pltpu.SemaphoreType.DMA((HALF,)),
        pltpu.SemaphoreType.DMA((HALF,)),
        pltpu.SemaphoreType.DMA((HALF,)),
        pltpu.SemaphoreType.DMA((3,)),
        pltpu.SemaphoreType.DMA((2,)),
        pltpu.SemaphoreType.DMA((2,)),
        pltpu.SemaphoreType.DMA((2,)),
        pltpu.SemaphoreType.DMA((3,)),
        pltpu.SemaphoreType.DMA((ndp,)),
        pltpu.SemaphoreType.DMA((ndp,)),
        pltpu.SemaphoreType.DMA((2,)),
        pltpu.SemaphoreType.DMA((3,)),
        pltpu.SemaphoreType.DMA((1,)),
        pltpu.SemaphoreType.DMA((GROUPS,)),
    ]
    turned = jnp.swapaxes(step_input, 2, 3)
    sent = pl.pallas_call(
        pair_kernel,
        name="mixer_tick",
        in_specs=[hbm] * 4 + [vmem] * 6,
        out_specs=[hbm] * 5,
        out_shape=[
            like(gate_input, BF16),
            like(conv_input, BF16),
            like(gate_input, BF16),
            like(turned, BF16),
            jax.ShapeDtypeStruct((2, HALF + 1, 8, MIX), F32),
        ],
        scratch_shapes=scratch,
        compiler_params=pltpu.CompilerParams(collective_id=0, has_side_effects=True),
    )(
        conv_input, gate_input, turned, cotangent, conv_weight,
        conv_bias, step_bias, decay_log, skip_gain, norm_gain,
    )
    done = pl.pallas_call(
        finish_kernel,
        name="mixer_finish",
        in_specs=[hbm] * 5,
        out_specs=[hbm] * 4 + [vmem] * 6,
        out_shape=[
            like(gate_input, BF16),
            like(conv_input, BF16),
            like(gate_input, BF16),
            like(turned, BF16),
            like(conv_weight, F32),
            like(conv_bias, F32),
            like(step_bias, F32),
            like(decay_log, F32),
            like(skip_gain, F32),
            like(norm_gain, F32),
        ],
        scratch_shapes=[
            pltpu.VMEM((7, tok, INNER), BF16),
            pltpu.VMEM((HEADS, tok), BF16),
            pltpu.VMEM((2, HALF + 1, 8, MIX), F32),
            pltpu.SemaphoreType.DMA((9,)),
            pltpu.SemaphoreType.DMA((8,)),
        ],
    )(*sent)
    return tuple(done[:3]) + (jnp.swapaxes(done[3], 2, 3),) + tuple(done[4:])


def solution(mesh):
    in_specs = (
        P("section", "dp", "ctx", None),
        P("section", "dp", "ctx", None),
        P("section", "dp", "ctx", None),
        P("section", "dp", "ctx", None),
        P("section", None, None),
        P("section", None),
        P("section", None),
        P("section", None),
        P("section", None),
        P("section", None),
    )
    out_specs = (
        P("section", "dp", "ctx", None),
        P("section", "dp", "ctx", None),
        P("section", "dp", "ctx", None),
        P("section", "dp", "ctx", None),
        P("section", None, None),
        P("section", None),
        P("section", None),
        P("section", None),
        P("section", None),
        P("section", None),
    )
    body = paired if (mesh.shape["ctx"], mesh.shape["section"]) == (2, 4) else shards
    return jax.shard_map(body, mesh=mesh, in_specs=in_specs, out_specs=out_specs, check_vma=False)
```
